32 devices in a mesh: energy: 8 (over z, x), tile: 4 (over y, core).
Axes of the slice: x: 2, y: 2, z: 4, core: 2. Of those that a mesh axis runs over, the one named last changes fastest.
Arguments:
- object_tiles: float32 [8, 2, 4, 512, 512], P('energy', None, 'tile'), may hold values from -6 to 6
- probe_wave: float32 [8, 2, 256, 256], P('energy'), may hold values from -6 to 6
- measured: bfloat16 [8, 4, 16, 256, 256], P('energy', 'tile'), may hold values from 0 to 2
- positions: int32 [4, 16, 2], P('tile'), may hold values from 0 to 511, as said below
- materials: float32 [2, 8, 8], replicated, may hold values from -6 to 6
Outputs:
- fitted: float32 [8, 2, 4, 512, 512], P('energy', None, 'tile')
The draws below stay inside these ranges and needn't reach their ends.
Inputs may be any that keep to these rules, and one draw needn't show every extreme that they name: `positions`: each entry is the corner of a 256 x 256 patch, given inside its tile; in every tile some patch has row corner 512 - 1 and some has column corner 512 - 1.
All inputs are finite; a program needn't handle non-finite values.
Results may differ from the reference program's by a relative error of at most 0.0013.
Values sent between devices are 32-bit elements; how exact they have to be, the bound alone decides.
A program may use at most 64 MiB of HBM per device.

```python
import math
import jax
import jax.numpy as jnp
from jax import lax

PATCH = 256
TILE_PX = 512
TILE_COLS = 4
PATCHES = 16
MATERIALS = 8
FIT_STEPS = 10
ENERGIES = 8
TILES = 4


def draw_positions(key, part):
    base = jax.random.fold_in(key, 11)
    row_key, col_key = jax.random.split(base)
    row_draw = jax.random.randint(row_key, (TILES, PATCHES), 0, TILE_PX, dtype=jnp.int32)
    col_draw = jax.random.randint(col_key, (TILES, PATCHES), 0, TILE_PX, dtype=jnp.int32)
    col_draw = col_draw.at[:, 0].set(TILE_PX - 1)
    row_draw = row_draw.at[:, 1].set(TILE_PX - 1)
    col_draw = col_draw.at[:, 1].set(TILE_PX - 1)
    corners = jnp.stack([row_draw, col_draw], -1).astype(jnp.int32)
    return corners


def steps_of(key, shape, cuts, smallest, top_value):
    def one(position, blocks):
        steps = jax.random.uniform(jax.random.fold_in(jax.random.fold_in(key, 6), position), (blocks,), jnp.float32, smallest / len(cuts), top_value / len(cuts))
        return jnp.repeat(jnp.exp(steps), shape[position] // blocks).reshape((-1,) + (1,) * (len(shape) - position - 1))

    gain = one(*cuts[0])
    for cut in cuts[1:]:
        gain = gain * one(*cut)
    return gain


def normal_values(stream_key, extent, width, limit, pieces=(), kind=jnp.bfloat16):
    level = steps_of(stream_key, extent, pieces, -0.22, 0.18) if pieces else 1.0
    entries = jax.random.normal(stream_key, extent, jnp.float32) * width * level
    return jnp.minimum(jnp.maximum(entries, -limit), limit).astype(kind)


def setup_inputs(seed: int = 0) -> dict:
    key_list = jax.random.split(jax.random.key(seed), 6)
    object_tiles = normal_values(key_list[0], (ENERGIES, 2, TILES, TILE_PX, TILE_PX), 1.0, 6.0, ((0, 8), (2, 4)), jnp.float32)
    probe_wave = normal_values(key_list[1], (ENERGIES, 2, PATCH, PATCH), 1.0, 6.0, ((0, 8),), jnp.float32)
    measured = jnp.clip(2.0 * jax.random.uniform(key_list[2], (ENERGIES, TILES, PATCHES, PATCH, PATCH), jnp.float32) ** steps_of(key_list[2], (ENERGIES, TILES, PATCHES, PATCH, PATCH), ((0, 8), (1, 4)), -0.2, 0.2), 0.0, 2.0).astype(jnp.bfloat16)
    positions = draw_positions(jax.random.fold_in(key_list[5], 71), 0)
    materials = normal_values(key_list[4], (2, ENERGIES, MATERIALS), 1.0, 6.0, (), jnp.float32)
    return {"object_tiles": object_tiles, "probe_wave": probe_wave, "measured": measured, "positions": positions, "materials": materials}


amplitude_floor = 0.5

def fourier_tables(length, direction):
    counter = jnp.arange(length, dtype=jnp.int32)
    products = counter[:, None] * counter[None, :] % length
    angles = 2.0 * math.pi / length * products.astype(jnp.float32)
    cosine = jnp.cos(angles)
    sine = direction * jnp.sin(angles)
    left_table = jnp.concatenate([jnp.concatenate([cosine, sine], 1), jnp.concatenate([-sine, cosine], 1)], 0).astype(jnp.bfloat16)
    right_table = jnp.concatenate([jnp.concatenate([cosine, -sine], 1), jnp.concatenate([sine, cosine], 1)], 0).astype(jnp.bfloat16)
    return (left_table, right_table)

def transform(real_part, imag_part, left_table, right_table):
    length = real_part.shape[0]
    stacked = jnp.concatenate([real_part, imag_part], 0).astype(jnp.bfloat16)
    inner = jnp.dot(left_table, stacked, preferred_element_type=jnp.float32)
    beside = jnp.concatenate([inner[:length], inner[length:]], 1).astype(jnp.bfloat16)
    outer = jnp.dot(beside, right_table, preferred_element_type=jnp.float32) / length
    return (outer[:, :length], outer[:, length:])

def patch_gradient(field_real, field_imag, probe_real, probe_imag, amplitude, row_start, col_start, tables):
    length = probe_real.shape[0]
    piece_real = lax.dynamic_slice(field_real, (row_start, col_start), (length, length))
    piece_imag = lax.dynamic_slice(field_imag, (row_start, col_start), (length, length))
    exit_real = probe_real * piece_real - probe_imag * piece_imag
    exit_imag = probe_real * piece_imag + probe_imag * piece_real
    far_real, far_imag = transform(exit_real, exit_imag, tables[0], tables[1])
    magnitude = jnp.sqrt(far_real * far_real + far_imag * far_imag)
    factor = amplitude.astype(jnp.float32) / jnp.maximum(magnitude, amplitude_floor) - 1.0
    back_real, back_imag = transform(factor * far_real, factor * far_imag, tables[2], tables[3])
    return (probe_real * back_real + probe_imag * back_imag, probe_real * back_imag - probe_imag * back_real)

def fit_materials(data, materials):
    high = lax.Precision.HIGHEST
    gram = jnp.einsum('rem,ren->mn', materials, materials, precision=high)
    rate = 1.0 / jnp.trace(gram)
    target = jnp.einsum('rem,rep->mp', materials, data, precision=high)

    def descend(number, coefficients):
        slope = jnp.dot(gram, coefficients, precision=high) - target
        return jnp.maximum(coefficients - rate * slope, 0.0)
    return lax.fori_loop(0, FIT_STEPS, descend, jnp.zeros_like(target))

def energy_update(object_one, probe_one, measured_one, positions):
    right_strip = jnp.roll(object_one, -1, axis=1)[:, :, :, :PATCH]
    widened = jnp.concatenate([object_one, right_strip], 3)
    lower_strip = jnp.roll(widened, -TILE_COLS, axis=1)[:, :, :PATCH, :]
    extended = jnp.concatenate([widened, lower_strip], 2)
    forward = fourier_tables(PATCH, 1.0)
    inverse = fourier_tables(PATCH, -1.0)
    tables = (forward[0], forward[1], inverse[0], inverse[1])
    flat_measured = measured_one.reshape(TILES * PATCHES, PATCH, PATCH)
    flat_corners = positions.reshape(TILES * PATCHES, 2)
    anchor = jnp.zeros((), jnp.int32)

    def accumulate(number, gradient):
        tile_index = (number // PATCHES).astype(jnp.int32)
        row_start = flat_corners[number, 0].astype(jnp.int32)
        col_start = flat_corners[number, 1].astype(jnp.int32)
        field = lax.dynamic_index_in_dim(extended, tile_index, 1, False)
        term_real, term_imag = patch_gradient(field[0], field[1], probe_one[0], probe_one[1], flat_measured[number], row_start, col_start, tables)
        current = lax.dynamic_slice(gradient, (anchor, tile_index, row_start, col_start), (2, 1, PATCH, PATCH))
        added = current + jnp.stack([term_real, term_imag])[:, None]
        return lax.dynamic_update_slice(gradient, added, (anchor, tile_index, row_start, col_start))
    gradient = lax.fori_loop(0, TILES * PATCHES, accumulate, jnp.zeros_like(extended))
    from_above = jnp.roll(gradient[:, :, TILE_PX:, :], TILE_COLS, axis=1)
    upper = jnp.concatenate([gradient[:, :, :PATCH, :] + from_above, gradient[:, :, PATCH:TILE_PX, :]], 2)
    from_left = jnp.roll(upper[:, :, :, TILE_PX:], 1, axis=1)
    summed = jnp.concatenate([upper[:, :, :, :PATCH] + from_left, upper[:, :, :, PATCH:TILE_PX]], 3)
    peak = jnp.max(probe_one[0] * probe_one[0] + probe_one[1] * probe_one[1])
    return object_one + summed / peak

def reference(object_tiles, probe_wave, measured, positions, materials):
    updated = lax.map(lambda inputs: energy_update(inputs[0], inputs[1], inputs[2], positions), (object_tiles, probe_wave, measured))
    data = updated.transpose(1, 0, 2, 3, 4).reshape(2, ENERGIES, TILES * TILE_PX * TILE_PX)
    coefficients = fit_materials(data, materials)
    spectra = jnp.einsum('rem,mp->rep', materials, coefficients, precision=lax.Precision.HIGHEST)
    spectra = spectra.reshape(2, ENERGIES, TILES, TILE_PX, TILE_PX).transpose(1, 0, 2, 3, 4)
    return spectra
```

```python
import functools
import math

import jax
import jax.numpy as jnp
import numpy as np
from jax import lax
from jax.experimental import pallas as pl
from jax.experimental.pallas import tpu as pltpu
from jax.sharding import PartitionSpec as P

TILE_COLS = 4
FIT_STEPS = 10
LANES = 128


amplitude_floor = 0.5


def shifted(value, axis, steps):
    count = lax.axis_size(axis)
    pairs = [(source, (source + steps) % count) for source in range(count)]
    return lax.ppermute(value, axis, pairs)


def fourier_parts(length):
    counter = np.arange(length, dtype=np.int64)
    angles = 2.0 * math.pi / length * (counter[:, None] * counter[None, :] % length)
    return (
        jnp.asarray(np.cos(angles), jnp.float32).astype(jnp.bfloat16),
        jnp.asarray(np.sin(angles), jnp.float32).astype(jnp.bfloat16),
    )


def joined(top_left, top_right, bottom_left, bottom_right):
    return jnp.concatenate(
        [
            jnp.concatenate([top_left, top_right], 1),
            jnp.concatenate([bottom_left, bottom_right], 1),
        ],
        0,
    )


def transform(real_part, imag_part, left_ref, right_ref):
    length = real_part.shape[0]
    stacked = jnp.concatenate([real_part.astype(jnp.bfloat16), imag_part.astype(jnp.bfloat16)], 0)
    inner = jnp.dot(left_ref[...], stacked, preferred_element_type=jnp.float32)
    inner = inner.astype(jnp.bfloat16)
    beside = jnp.concatenate([inner[:length], inner[length:]], 1)
    outer = jnp.dot(beside, right_ref[...], preferred_element_type=jnp.float32) * (1.0 / length)
    return outer[:, :length], outer[:, length:]


def window(ref, part, row, block, shift, length):
    lane = lax.broadcasted_iota(jnp.int32, (length, LANES), 1)
    back = lax.rem(LANES - shift, LANES)
    tiles = [
        pltpu.roll(ref[part, block + at, pl.ds(row, length), :], back, 1)
        for at in range(length // LANES + 1)
    ]
    keep = lane < LANES - shift
    return jnp.concatenate(
        [jnp.where(keep, one, other) for one, other in zip(tiles[:-1], tiles[1:])], 1
    )


def add_window(ref, part, row, block, shift, term):
    length = term.shape[0]
    lane = lax.broadcasted_iota(jnp.int32, (length, LANES), 1)
    tiles = [pltpu.roll(term[:, at : at + LANES], shift, 1) for at in range(0, length, LANES)]
    keep = lane >= shift
    zero = jnp.zeros_like(tiles[0])
    for at, (one, other) in enumerate(zip(tiles + [zero], [zero] + tiles)):
        place = (part, block + at, pl.ds(row, length), slice(None))
        ref[place] = ref[place] + jnp.where(keep, one, other)


def patch_kernel(
    fold,
    corners_ref,
    object_ref,
    right_ref,
    lower_ref,
    probe_ref,
    measured_ref,
    cosine_ref,
    sine_ref,
    main_out,
    side_out,
    below_out,
    field,
    gradient,
    tables,
    sems,
):
    tile_px = object_ref.shape[-1]
    length = probe_ref.shape[-1]
    count = measured_ref.shape[0]
    blocks = tile_px // LANES
    top = pl.ds(0, tile_px)
    bottom = pl.ds(tile_px, length)
    moves = []
    for block in range(blocks + length // LANES):
        ref, at = (object_ref, block) if block < blocks else (right_ref, block - blocks)
        columns = pl.ds(at * LANES, LANES)
        moves.append((ref.at[:, :, columns], field.at[:, block, top, :]))
        if fold:
            source = ref.at[:, pl.ds(0, length), columns]
        else:
            source = lower_ref.at[:, :, pl.ds(block * LANES, LANES)]
        moves.append((source, field.at[:, block, bottom, :]))
    copies = [
        pltpu.make_async_copy(source, target, sems.at[number])
        for number, (source, target) in enumerate(moves)
    ]
    for copy in copies:
        copy.start()
    cosine = cosine_ref[...]
    sine = sine_ref[...]
    tables[0] = joined(cosine, sine, -sine, cosine)
    tables[1] = joined(cosine, -sine, sine, cosine)
    gradient[...] = jnp.zeros_like(gradient)
    for copy in copies:
        copy.wait()

    def step(number, carry):
        row = corners_ref[number, 0]
        col = corners_ref[number, 1]
        block = col // LANES
        shift = col - block * LANES
        piece_real = window(field, 0, row, block, shift, length)
        piece_imag = window(field, 1, row, block, shift, length)
        probe_real = probe_ref[0]
        probe_imag = probe_ref[1]
        exit_real = probe_real * piece_real - probe_imag * piece_imag
        exit_imag = probe_real * piece_imag + probe_imag * piece_real
        far_real, far_imag = transform(exit_real, exit_imag, tables.at[0], tables.at[1])
        square = far_real * far_real + far_imag * far_imag
        scale = lax.rsqrt(jnp.maximum(square, amplitude_floor * amplitude_floor))
        factor = measured_ref[number].astype(jnp.float32) * scale - 1.0
        back_real, back_imag = transform(
            factor * far_real, factor * far_imag, tables.at[1], tables.at[0]
        )
        probe_real = probe_ref[0]
        probe_imag = probe_ref[1]
        add_window(
            gradient, 0, row, block, shift, probe_real * back_real + probe_imag * back_imag
        )
        add_window(
            gradient, 1, row, block, shift, probe_real * back_imag - probe_imag * back_real
        )
        return carry

    lax.fori_loop(0, count, step, 0)
    peak = jnp.max(probe_ref[0] * probe_ref[0] + probe_ref[1] * probe_ref[1])
    rows = 64

    def finish(wrapped, number, carry):
        place = (pl.ds(pl.multiple_of(number * rows, rows), rows), slice(None))
        beyond = pl.ds(pl.multiple_of(tile_px + number * rows, rows), rows)
        for part in range(2):
            for block in range(blocks + length // LANES):
                total = gradient[(part, block) + place]
                if wrapped:
                    total = total + gradient[part, block, beyond, :]
                share = total / peak
                if block < blocks:
                    columns = slice(block * LANES, (block + 1) * LANES)
                    main_out[part, place[0], columns] = field[(part, block) + place] + share
                else:
                    columns = slice((block - blocks) * LANES, (block - blocks + 1) * LANES)
                    side_out[part, place[0], columns] = share
        return carry

    lax.fori_loop(0, length // rows, functools.partial(finish, fold), 0)
    lax.fori_loop(length // rows, tile_px // rows, functools.partial(finish, False), 0)
    if fold:
        below_out[...] = jnp.zeros_like(below_out)
    else:
        for block in range(blocks + length // LANES):
            columns = slice(block * LANES, (block + 1) * LANES)
            below_out[:, :, columns] = gradient[:, block, tile_px:, :] / peak


def patch_update(own_object, right_strip, lower_strip, probe, measured, corners, fold):
    tile_px = own_object.shape[-1]
    length = probe.shape[-1]
    count = measured.shape[0]
    width = tile_px + length
    cosine, sine = fourier_parts(length)
    below = (2, 8, LANES) if fold else (2, length, width)
    vmem = pl.BlockSpec(memory_space=pltpu.VMEM)
    anywhere = pl.BlockSpec(memory_space=pl.ANY)
    return pl.pallas_call(
        functools.partial(patch_kernel, fold),
        out_shape=(
            jax.ShapeDtypeStruct((2, tile_px, tile_px), jnp.float32),
            jax.ShapeDtypeStruct((2, tile_px, length), jnp.float32),
            jax.ShapeDtypeStruct(below, jnp.float32),
        ),
        in_specs=[
            pl.BlockSpec(memory_space=pltpu.SMEM),
            anywhere,
            anywhere,
            anywhere,
            vmem,
            vmem,
            vmem,
            vmem,
        ],
        out_specs=(vmem, vmem, vmem),
        scratch_shapes=[
            pltpu.VMEM((2, width // LANES, width, LANES), jnp.float32),
            pltpu.VMEM((2, width // LANES, width, LANES), jnp.float32),
            pltpu.VMEM((2, 2 * length, 2 * length), jnp.bfloat16),
            pltpu.SemaphoreType.DMA((2 * (width // LANES),)),
        ],
        compiler_params=pltpu.CompilerParams(vmem_limit_bytes=48 * 1024 * 1024),
        cost_estimate=pl.CostEstimate(
            flops=64 * count * length**3, bytes_accessed=16 * tile_px * tile_px, transcendentals=0
        ),
        name="patches",
    )(corners, own_object, right_strip, lower_strip, probe, measured, cosine, sine)


def fit_scalars(materials_ref, energies, kinds):
    spectra = [
        [materials_ref[(part * energies + energy) * kinds + kind] for kind in range(kinds)]
        for part in range(2)
        for energy in range(energies)
    ]
    gram = [[None] * kinds for _ in range(kinds)]
    for one in range(kinds):
        for other in range(one, kinds):
            total = spectra[0][one] * spectra[0][other]
            for row in spectra[1:]:
                total = total + row[one] * row[other]
            gram[one][other] = total
            gram[other][one] = total
    trace = gram[0][0]
    for one in range(1, kinds):
        trace = trace + gram[one][one]
    return gram, trace


def fit_kernel(materials_ref, data_ref, out_ref, step_ref):
    energies, rows, width = data_ref.shape[1:]
    kinds = materials_ref.shape[0] // (2 * energies)
    gram, trace = fit_scalars(materials_ref, energies, kinds)
    rate = 1.0 / trace
    for one in range(kinds):
        for other in range(kinds):
            unit = 1.0 if one == other else 0.0
            step_ref[one * kinds + other] = unit - rate * gram[one][other]
    tall, wide = 8, 256
    across = width // wide
    pairs = [(part, energy) for part in range(2) for energy in range(energies)]

    def chunk(number, carry):
        row = pl.multiple_of(number // across * tall, tall)
        col = pl.multiple_of(number % across * wide, wide)
        place = (pl.ds(row, tall), pl.ds(col, wide))
        target = [None] * kinds
        for part, energy in pairs:
            plane = data_ref[(part, energy) + place]
            for kind in range(kinds):
                term = materials_ref[(part * energies + energy) * kinds + kind] * plane
                target[kind] = term if target[kind] is None else target[kind] + term
        target = [rate * value for value in target]
        current = [jnp.maximum(value, 0.0) for value in target]

        def descend(turn, current):
            following = []
            for one in range(kinds):
                total = target[one]
                for other in range(kinds):
                    total = total + step_ref[one * kinds + other] * current[other]
                following.append(jnp.maximum(total, 0.0))
            return following

        current = lax.fori_loop(1, FIT_STEPS, descend, current)
        for part, energy in pairs:
            total = None
            for kind in range(kinds):
                term = materials_ref[(part * energies + energy) * kinds + kind] * current[kind]
                total = term if total is None else total + term
            out_ref[(part, energy) + place] = total
        return carry

    lax.fori_loop(0, rows // tall * across, chunk, 0)


def fit_spectra(data, materials):
    kinds = materials.shape[-1]
    vmem = pl.BlockSpec(memory_space=pltpu.VMEM)
    return pl.pallas_call(
        fit_kernel,
        out_shape=jax.ShapeDtypeStruct(data.shape, jnp.float32),
        in_specs=[pl.BlockSpec(memory_space=pltpu.SMEM), vmem],
        out_specs=vmem,
        scratch_shapes=[pltpu.SMEM((kinds * kinds,), jnp.float32)],
        name="fit",
    )(materials.reshape(-1), data)


def body(object_tiles, probe_wave, measured, positions, materials):
    own_object = object_tiles[0, :, 0]
    tile_px = own_object.shape[-1]
    length = probe_wave.shape[-1]
    tile_count = lax.axis_size("tile")
    row_step = TILE_COLS % tile_count
    fold = row_step == 0
    right_strip = shifted(own_object[:, :, :length], "tile", -1)
    if fold:
        lower_strip = jnp.zeros((2, 8, LANES), jnp.float32)
    else:
        widened = jnp.concatenate([own_object[:, :length], right_strip[:, :length]], 2)
        lower_strip = shifted(widened, "tile", -row_step)
    main, side, below = patch_update(
        own_object, right_strip, lower_strip, probe_wave[0], measured[0, 0], positions[0], fold
    )
    if not fold:
        from_above = shifted(below, "tile", row_step)
        main = main.at[:, :length, :].add(from_above[:, :, :tile_px])
        side = side.at[:, :length, :].add(from_above[:, :, tile_px:])
    from_left = shifted(side, "tile", 1)
    updated = jnp.concatenate([main[:, :, :length] + from_left, main[:, :, length:]], 2)
    groups = lax.axis_size("energy")
    group_rows = tile_px // groups
    outgoing = updated.reshape(2, groups, group_rows, tile_px)
    arrived = lax.all_to_all(outgoing, "energy", split_axis=1, concat_axis=1, tiled=True)
    spectra = fit_spectra(arrived, materials)
    returned = lax.all_to_all(spectra, "energy", split_axis=1, concat_axis=1, tiled=True)
    return returned.reshape(1, 2, 1, tile_px, tile_px)


def solution(mesh):
    in_specs = (
        P("energy", None, "tile", None, None),
        P("energy", None, None, None),
        P("energy", "tile", None, None, None),
        P("tile", None, None),
        P(),
    )
    out_specs = P("energy", None, "tile", None, None)
    return jax.shard_map(body, mesh=mesh, in_specs=in_specs, out_specs=out_specs, check_vma=False)
```

```python
import functools
import math

import jax
import jax.numpy as jnp
import numpy as np
from jax import lax
from jax.experimental import pallas as pl
from jax.experimental.pallas import tpu as pltpu
from jax.sharding import PartitionSpec as P

TILE_COLS = 4
FIT_STEPS = 10
LANES = 128


amplitude_floor = 0.5


def shifted(value, axis, steps):
    count = lax.axis_size(axis)
    pairs = [(source, (source + steps) % count) for source in range(count)]
    return lax.ppermute(value, axis, pairs)


def fourier_parts(length):
    counter = np.arange(length, dtype=np.int64)
    angles = 2.0 * math.pi / length * (counter[:, None] * counter[None, :] % length)
    return (
        jnp.asarray(np.cos(angles), jnp.float32).astype(jnp.bfloat16),
        jnp.asarray(np.sin(angles), jnp.float32).astype(jnp.bfloat16),
    )


def joined(top_left, top_right, bottom_left, bottom_right):
    return jnp.concatenate(
        [
            jnp.concatenate([top_left, top_right], 1),
            jnp.concatenate([bottom_left, bottom_right], 1),
        ],
        0,
    )


def transform(real_part, imag_part, left_ref, right_ref):
    length = real_part.shape[0]
    stacked = jnp.concatenate([real_part.astype(jnp.bfloat16), imag_part.astype(jnp.bfloat16)], 0)
    inner = jnp.dot(left_ref[...], stacked, preferred_element_type=jnp.float32)
    inner = inner.astype(jnp.bfloat16)
    beside = jnp.concatenate([inner[:length], inner[length:]], 1)
    outer = jnp.dot(beside, right_ref[...], preferred_element_type=jnp.float32) * (1.0 / length)
    return outer[:, :length], outer[:, length:]


def window(ref, part, row, block, shift, length):
    lane = lax.broadcasted_iota(jnp.int32, (length, LANES), 1)
    back = lax.rem(LANES - shift, LANES)
    tiles = [
        pltpu.roll(ref[part, block + at, pl.ds(row, length), :], back, 1)
        for at in range(length // LANES + 1)
    ]
    keep = lane < LANES - shift
    return jnp.concatenate(
        [jnp.where(keep, one, other) for one, other in zip(tiles[:-1], tiles[1:])], 1
    )


def add_window(ref, part, row, block, shift, term):
    length = term.shape[0]
    lane = lax.broadcasted_iota(jnp.int32, (length, LANES), 1)
    tiles = [pltpu.roll(term[:, at : at + LANES], shift, 1) for at in range(0, length, LANES)]
    keep = lane >= shift
    zero = jnp.zeros_like(tiles[0])
    for at, (one, other) in enumerate(zip(tiles + [zero], [zero] + tiles)):
        place = (part, block + at, pl.ds(row, length), slice(None))
        ref[place] = ref[place] + jnp.where(keep, one, other)


def patch_kernel(
    fold,
    corners_ref,
    object_ref,
    right_ref,
    lower_ref,
    probe_ref,
    measured_ref,
    cosine_ref,
    sine_ref,
    main_out,
    side_out,
    below_out,
    field,
    gradient,
    tables,
    sems,
):
    tile_px = object_ref.shape[-1]
    length = probe_ref.shape[-1]
    count = measured_ref.shape[0]
    blocks = tile_px // LANES
    top = pl.ds(0, tile_px)
    bottom = pl.ds(tile_px, length)
    moves = []
    for block in range(blocks + length // LANES):
        ref, at = (object_ref, block) if block < blocks else (right_ref, block - blocks)
        columns = pl.ds(at * LANES, LANES)
        moves.append((ref.at[:, :, columns], field.at[:, block, top, :]))
        if fold:
            source = ref.at[:, pl.ds(0, length), columns]
        else:
            source = lower_ref.at[:, :, pl.ds(block * LANES, LANES)]
        moves.append((source, field.at[:, block, bottom, :]))
    copies = [
        pltpu.make_async_copy(source, target, sems.at[number])
        for number, (source, target) in enumerate(moves)
    ]
    for copy in copies:
        copy.start()
    cosine = cosine_ref[...]
    sine = sine_ref[...]
    tables[0] = joined(cosine, sine, -sine, cosine)
    tables[1] = joined(cosine, -sine, sine, cosine)
    gradient[...] = jnp.zeros_like(gradient)
    for copy in copies:
        copy.wait()

    def step(number, carry):
        row = corners_ref[number, 0]
        col = corners_ref[number, 1]
        block = col // LANES
        shift = col - block * LANES
        piece_real = window(field, 0, row, block, shift, length)
        piece_imag = window(field, 1, row, block, shift, length)
        probe_real = probe_ref[0]
        probe_imag = probe_ref[1]
        exit_real = probe_real * piece_real - probe_imag * piece_imag
        exit_imag = probe_real * piece_imag + probe_imag * piece_real
        far_real, far_imag = transform(exit_real, exit_imag, tables.at[0], tables.at[1])
        square = far_real * far_real + far_imag * far_imag
        scale = lax.rsqrt(jnp.maximum(square, amplitude_floor * amplitude_floor))
        factor = measured_ref[number].astype(jnp.float32) * scale - 1.0
        back_real, back_imag = transform(
            factor * far_real, factor * far_imag, tables.at[1], tables.at[0]
        )
        probe_real = probe_ref[0]
        probe_imag = probe_ref[1]
        add_window(
            gradient, 0, row, block, shift, probe_real * back_real + probe_imag * back_imag
        )
        add_window(
            gradient, 1, row, block, shift, probe_real * back_imag - probe_imag * back_real
        )
        return carry

    lax.fori_loop(0, count, step, 0)
    peak = jnp.max(probe_ref[0] * probe_ref[0] + probe_ref[1] * probe_ref[1])
    rows = 64

    def finish(wrapped, number, carry):
        place = (pl.ds(pl.multiple_of(number * rows, rows), rows), slice(None))
        beyond = pl.ds(pl.multiple_of(tile_px + number * rows, rows), rows)
        for part in range(2):
            for block in range(blocks + length // LANES):
                total = gradient[(part, block) + place]
                if wrapped:
                    total = total + gradient[part, block, beyond, :]
                share = total / peak
                if block < blocks:
                    columns = slice(block * LANES, (block + 1) * LANES)
                    main_out[part, place[0], columns] = field[(part, block) + place] + share
                else:
                    columns = slice((block - blocks) * LANES, (block - blocks + 1) * LANES)
                    side_out[part, place[0], columns] = share
        return carry

    lax.fori_loop(0, length // rows, functools.partial(finish, fold), 0)
    lax.fori_loop(length // rows, tile_px // rows, functools.partial(finish, False), 0)
    if fold:
        below_out[...] = jnp.zeros_like(below_out)
    else:
        for block in range(blocks + length // LANES):
            columns = slice(block * LANES, (block + 1) * LANES)
            below_out[:, :, columns] = gradient[:, block, tile_px:, :] / peak


def patch_update(own_object, right_strip, lower_strip, probe, measured, corners, fold):
    tile_px = own_object.shape[-1]
    length = probe.shape[-1]
    count = measured.shape[0]
    width = tile_px + length
    cosine, sine = fourier_parts(length)
    below = (2, 8, LANES) if fold else (2, length, width)
    vmem = pl.BlockSpec(memory_space=pltpu.VMEM)
    anywhere = pl.BlockSpec(memory_space=pl.ANY)
    return pl.pallas_call(
        functools.partial(patch_kernel, fold),
        out_shape=(
            jax.ShapeDtypeStruct((2, tile_px, tile_px), jnp.float32),
            jax.ShapeDtypeStruct((2, tile_px, length), jnp.float32),
            jax.ShapeDtypeStruct(below, jnp.float32),
        ),
        in_specs=[
            pl.BlockSpec(memory_space=pltpu.SMEM),
            anywhere,
            anywhere,
            anywhere,
            vmem,
            vmem,
            vmem,
            vmem,
        ],
        out_specs=(vmem, vmem, vmem),
        scratch_shapes=[
            pltpu.VMEM((2, width // LANES, width, LANES), jnp.float32),
            pltpu.VMEM((2, width // LANES, width, LANES), jnp.float32),
            pltpu.VMEM((2, 2 * length, 2 * length), jnp.bfloat16),
            pltpu.SemaphoreType.DMA((2 * (width // LANES),)),
        ],
        compiler_params=pltpu.CompilerParams(vmem_limit_bytes=48 * 1024 * 1024),
        cost_estimate=pl.CostEstimate(
            flops=64 * count * length**3, bytes_accessed=16 * tile_px * tile_px, transcendentals=0
        ),
        name="patches",
    )(corners, own_object, right_strip, lower_strip, probe, measured, cosine, sine)


def fit_scalars(materials_ref, energies, kinds):
    spectra = [
        [materials_ref[(part * energies + energy) * kinds + kind] for kind in range(kinds)]
        for part in range(2)
        for energy in range(energies)
    ]
    gram = [[None] * kinds for _ in range(kinds)]
    for one in range(kinds):
        for other in range(one, kinds):
            total = spectra[0][one] * spectra[0][other]
            for row in spectra[1:]:
                total = total + row[one] * row[other]
            gram[one][other] = total
            gram[other][one] = total
    trace = gram[0][0]
    for one in range(1, kinds):
        trace = trace + gram[one][one]
    return gram, trace


def fit_columns(materials_ref, step_ref, data, spectra, energies, kinds, rate, begin, wide):
    rows = data.shape[2]
    tall = 16 if rows % 16 == 0 else 8
    pairs = [(part, energy) for part in range(2) for energy in range(energies)]

    def chunk(number, carry):
        row = pl.multiple_of(number * tall, tall)
        place = (pl.ds(row, tall), pl.ds(begin, wide))
        target = [None] * kinds
        for part, energy in pairs:
            plane = data[(part, energy) + place]
            for kind in range(kinds):
                term = materials_ref[(part * energies + energy) * kinds + kind] * plane
                target[kind] = term if target[kind] is None else target[kind] + term
        target = [rate * value for value in target]
        current = [jnp.maximum(value, 0.0) for value in target]

        def descend(turn, current):
            following = []
            for one in range(kinds):
                total = target[one]
                for other in range(kinds):
                    total = total + step_ref[one * kinds + other] * current[other]
                following.append(jnp.maximum(total, 0.0))
            return following

        current = lax.fori_loop(1, FIT_STEPS, descend, current)
        for part, energy in pairs:
            total = None
            for kind in range(kinds):
                term = materials_ref[(part * energies + energy) * kinds + kind] * current[kind]
                total = term if total is None else total + term
            spectra[(part, energy) + place] = total
        return carry

    lax.fori_loop(0, rows // tall, chunk, 0)


def exchange_kernel(
    groups,
    tiles,
    materials_ref,
    main_ref,
    side_ref,
    out_ref,
    step_ref,
    margin,
    left,
    data,
    spectra,
    margin_sems,
    send_sems,
    recv_sems,
    own_sems,
):
    mesh_ids = pl.DeviceIdType.MESH
    me = lax.axis_index("energy")
    tile = lax.axis_index("tile")
    after = lax.rem(tile + 1, tiles)
    before = lax.rem(tile + tiles - 1, tiles)
    tile_px = main_ref.shape[-1]
    length = side_ref.shape[-1]
    rows = tile_px // groups
    kinds = materials_ref.shape[0] // (2 * groups)
    offsets = sorted(range(1, groups), key=lambda offset: abs(offset - groups // 2))
    peers = {offset: lax.rem(me + offset, groups) for offset in offsets}

    barrier = pltpu.get_barrier_semaphore()
    for neighbour in (after, before):
        pl.semaphore_signal(barrier, inc=1, device_id=(me, neighbour), device_id_type=mesh_ids)
    for offset in offsets:
        pl.semaphore_signal(
            barrier, inc=1, device_id=(peers[offset], tile), device_id_type=mesh_ids
        )

    gram, trace = fit_scalars(materials_ref, groups, kinds)
    rate = 1.0 / trace
    for one in range(kinds):
        for other in range(kinds):
            unit = 1.0 if one == other else 0.0
            step_ref[one * kinds + other] = unit - rate * gram[one][other]
    pl.semaphore_wait(barrier, groups + 1)

    margin_copy = pltpu.make_async_remote_copy(
        src_ref=side_ref,
        dst_ref=margin,
        send_sem=margin_sems.at[0],
        recv_sem=margin_sems.at[1],
        device_id=(me, after),
        device_id_type=mesh_ids,
    )
    margin_copy.start()

    def rows_of(group):
        return pl.ds(pl.multiple_of(group * rows, rows), rows)

    def outward(block):
        columns = pl.ds(block * LANES, LANES)
        source = left if block * LANES < length else main_ref
        copies = [
            pltpu.make_async_remote_copy(
                src_ref=source.at[:, rows_of(peers[offset]), columns],
                dst_ref=data.at[:, me, :, columns],
                send_sem=send_sems.at[0, block, offset],
                recv_sem=recv_sems.at[0, block, offset],
                device_id=(peers[offset], tile),
                device_id_type=mesh_ids,
            )
            for offset in offsets
        ]
        own = pltpu.make_async_copy(
            source.at[:, rows_of(me), columns], data.at[:, me, :, columns], own_sems.at[0, block]
        )
        return copies, own

    def homeward(block):
        columns = pl.ds(block * LANES, LANES)
        copies = [
            pltpu.make_async_remote_copy(
                src_ref=spectra.at[:, peers[offset], :, columns],
                dst_ref=out_ref.at[:, rows_of(me), columns],
                send_sem=send_sems.at[1, block, offset],
                recv_sem=recv_sems.at[1, block, offset],
                device_id=(peers[offset], tile),
                device_id_type=mesh_ids,
            )
            for offset in offsets
        ]
        own = pltpu.make_async_copy(
            spectra.at[:, me, :, columns], out_ref.at[:, rows_of(me), columns], own_sems.at[1, block]
        )
        return copies, own

    def start(moves):
        for copy in moves[0]:
            copy.start()
        moves[1].start()

    blocks = tile_px // LANES
    early = [block for block in range(blocks) if block * LANES >= length]
    late = [block for block in range(blocks) if block * LANES < length]
    going = {}
    for block in early:
        going[block] = outward(block)
        start(going[block])
    margin_copy.wait()
    for block in late:
        columns = slice(block * LANES, (block + 1) * LANES)
        left[:, :, columns] = main_ref[:, :, columns] + margin[:, :, columns]
    for block in late:
        going[block] = outward(block)
        start(going[block])
    coming = {}
    for block in early + late:
        copies, own = going[block]
        for copy in copies:
            copy.wait_recv()
        own.wait()
        fit_columns(
            materials_ref, step_ref, data, spectra, groups, kinds, rate, block * LANES, LANES
        )
        coming[block] = homeward(block)
        start(coming[block])
    for block in early + late:
        for copy in going[block][0]:
            copy.wait_send()
        copies, own = coming[block]
        own.wait()
        for copy in copies:
            copy.wait()


def exchange_fit(main, side, materials):
    groups = lax.axis_size("energy")
    tiles = lax.axis_size("tile")
    tile_px = main.shape[-1]
    length = side.shape[-1]
    kinds = materials.shape[-1]
    rows = tile_px // groups
    blocks = tile_px // LANES
    vmem = pl.BlockSpec(memory_space=pltpu.VMEM)
    return pl.pallas_call(
        functools.partial(exchange_kernel, groups, tiles),
        out_shape=jax.ShapeDtypeStruct(main.shape, jnp.float32),
        in_specs=[pl.BlockSpec(memory_space=pltpu.SMEM), vmem, vmem],
        out_specs=vmem,
        scratch_shapes=[
            pltpu.SMEM((kinds * kinds,), jnp.float32),
            pltpu.VMEM((2, tile_px, length), jnp.float32),
            pltpu.VMEM((2, tile_px, length), jnp.float32),
            pltpu.VMEM((2, groups, rows, tile_px), jnp.float32),
            pltpu.VMEM((2, groups, rows, tile_px), jnp.float32),
            pltpu.SemaphoreType.DMA((2,)),
            pltpu.SemaphoreType.DMA((2, blocks, groups)),
            pltpu.SemaphoreType.DMA((2, blocks, groups)),
            pltpu.SemaphoreType.DMA((2, blocks)),
        ],
        compiler_params=pltpu.CompilerParams(
            collective_id=0, has_side_effects=True, vmem_limit_bytes=32 * 1024 * 1024
        ),
        name="exchange",
    )(materials.reshape(-1), main, side)


def body(object_tiles, probe_wave, measured, positions, materials):
    own_object = object_tiles[0, :, 0]
    tile_px = own_object.shape[-1]
    length = probe_wave.shape[-1]
    tile_count = lax.axis_size("tile")
    row_step = TILE_COLS % tile_count
    fold = row_step == 0
    right_strip = shifted(own_object[:, :, :length], "tile", -1)
    if fold:
        lower_strip = jnp.zeros((2, 8, LANES), jnp.float32)
    else:
        widened = jnp.concatenate([own_object[:, :length], right_strip[:, :length]], 2)
        lower_strip = shifted(widened, "tile", -row_step)
    main, side, below = patch_update(
        own_object, right_strip, lower_strip, probe_wave[0], measured[0, 0], positions[0], fold
    )
    if not fold:
        from_above = shifted(below, "tile", row_step)
        main = main.at[:, :length, :].add(from_above[:, :, :tile_px])
        side = side.at[:, :length, :].add(from_above[:, :, tile_px:])
    fitted = exchange_fit(main, side, materials)
    return fitted.reshape(1, 2, 1, tile_px, tile_px)


def solution(mesh):
    in_specs = (
        P("energy", None, "tile", None, None),
        P("energy", None, None, None),
        P("energy", "tile", None, None, None),
        P("tile", None, None),
        P(),
    )
    out_specs = P("energy", None, "tile", None, None)
    return jax.shard_map(body, mesh=mesh, in_specs=in_specs, out_specs=out_specs, check_vma=False)
```

```python
import functools
import math

import jax
import jax.numpy as jnp
import numpy as np
from jax import lax
from jax.experimental import pallas as pl
from jax.experimental.pallas import tpu as pltpu
from jax.sharding import PartitionSpec as P

TILE_COLS = 4
FIT_STEPS = 10
LANES = 128


amplitude_floor = 0.5


def shifted(value, axis, steps):
    count = lax.axis_size(axis)
    pairs = [(source, (source + steps) % count) for source in range(count)]
    return lax.ppermute(value, axis, pairs)


def fourier_parts(length):
    counter = np.arange(length, dtype=np.int64)
    angles = 2.0 * math.pi / length * (counter[:, None] * counter[None, :] % length)
    return (
        jnp.asarray(np.cos(angles), jnp.float32).astype(jnp.bfloat16),
        jnp.asarray(np.sin(angles), jnp.float32).astype(jnp.bfloat16),
    )


def joined(top_left, top_right, bottom_left, bottom_right):
    return jnp.concatenate(
        [
            jnp.concatenate([top_left, top_right], 1),
            jnp.concatenate([bottom_left, bottom_right], 1),
        ],
        0,
    )


def transform(stacked, left_ref, right_ref):
    length = stacked.shape[0] // 2
    inner = jnp.dot(left_ref[...], stacked, preferred_element_type=jnp.float32)
    inner = inner.astype(jnp.bfloat16)
    beside = jnp.concatenate([inner[:length], inner[length:]], 1)
    outer = jnp.dot(beside, right_ref[...], preferred_element_type=jnp.float32) * (1.0 / length)
    return outer[:, :length], outer[:, length:]


def window(ref, part, row, block, shift, length):
    lane = lax.broadcasted_iota(jnp.int32, (length, LANES), 1)
    back = lax.rem(LANES - shift, LANES)
    tiles = [
        pltpu.roll(ref[part, block + at, pl.ds(row, length), :], back, 1)
        for at in range(length // LANES + 1)
    ]
    keep = lane < LANES - shift
    return jnp.concatenate(
        [jnp.where(keep, one, other) for one, other in zip(tiles[:-1], tiles[1:])], 1
    )


def add_window(ref, part, row, block, shift, term):
    length = term.shape[0]
    lane = lax.broadcasted_iota(jnp.int32, (length, LANES), 1)
    tiles = [pltpu.roll(term[:, at : at + LANES], shift, 1) for at in range(0, length, LANES)]
    keep = lane >= shift
    zero = jnp.zeros_like(tiles[0])
    for at, (one, other) in enumerate(zip(tiles + [zero], [zero] + tiles)):
        place = (part, block + at, pl.ds(row, length), slice(None))
        ref[place] = ref[place] + jnp.where(keep, one, other)


def patch_kernel(fold, inner, *refs):
    corners_ref, object_ref, measured_ref, probe_ref, cosine_ref, sine_ref = refs[:6]
    if inner:
        (gradient,) = refs[6:7]
        right_ref = lower_ref = None
        rest = refs[7:]
    else:
        right_ref, lower_ref, begun_ref, main_out, side_out, below_out = refs[6:12]
        gradient, *rest = refs[12:]
    field, tables, wave, terms, order, sems = rest
    tile_px = object_ref.shape[-1]
    length = probe_ref.shape[-1]
    count = measured_ref.shape[0]
    blocks = tile_px // LANES
    width = blocks + length // LANES
    top = pl.ds(0, tile_px)
    bottom = pl.ds(tile_px, length)
    moves = []
    for block in range(blocks if inner else width):
        ref, at = (object_ref, block) if block < blocks else (right_ref, block - blocks)
        columns = pl.ds(at * LANES, LANES)
        moves.append((ref.at[:, :, columns], field.at[:, block, top, :]))
        if fold:
            source = ref.at[:, pl.ds(0, length), columns]
        elif not inner:
            source = lower_ref.at[:, :, pl.ds(block * LANES, LANES)]
        else:
            continue
        moves.append((source, field.at[:, block, bottom, :]))
    copies = [
        pltpu.make_async_copy(source, target, sems.at[number])
        for number, (source, target) in enumerate(moves)
    ]
    for copy in copies:
        copy.start()
    cosine = cosine_ref[...]
    sine = sine_ref[...]
    tables[0] = joined(cosine, sine, -sine, cosine)
    tables[1] = joined(cosine, -sine, sine, cosine)
    if inner:
        gradient[...] = jnp.zeros_like(gradient)
    else:
        gradient[...] = begun_ref[...]
    terms[...] = jnp.zeros_like(terms)

    limit = tile_px - length

    def choose(number, found):
        order[found] = number
        within = corners_ref[number, 1] <= limit
        if not fold:
            within = jnp.logical_and(within, corners_ref[number, 0] <= limit)
        return found + jnp.where(within, int(inner), 1 - int(inner))

    total = lax.fori_loop(0, count, choose, 0)
    for copy in copies:
        copy.wait()

    def corner(turn):
        number = order[turn]
        row = corners_ref[number, 0]
        col = corners_ref[number, 1]
        block = col // LANES
        return number, row, block, col - block * LANES

    def gather(turn):
        _, row, block, shift = corner(turn)
        piece_real = window(field, 0, row, block, shift, length)
        piece_imag = window(field, 1, row, block, shift, length)
        probe_real = probe_ref[0]
        probe_imag = probe_ref[1]
        exit_real = probe_real * piece_real - probe_imag * piece_imag
        exit_imag = probe_real * piece_imag + probe_imag * piece_real
        wave[:length, :] = exit_real.astype(jnp.bfloat16)
        wave[length:, :] = exit_imag.astype(jnp.bfloat16)

    def scatter(turn):
        _, row, block, shift = corner(turn)
        add_window(gradient, 0, row, block, shift, terms[0])
        add_window(gradient, 1, row, block, shift, terms[1])

    def step(turn, carry):
        stacked = wave[...]
        scatter(jnp.maximum(turn - 1, 0))
        far_real, far_imag = transform(stacked, tables.at[0], tables.at[1])
        gather(jnp.minimum(turn + 1, total - 1))
        square = far_real * far_real + far_imag * far_imag
        scale = lax.rsqrt(jnp.maximum(square, amplitude_floor * amplitude_floor))
        factor = measured_ref[order[turn]].astype(jnp.float32) * scale - 1.0
        change = jnp.concatenate(
            [(factor * far_real).astype(jnp.bfloat16), (factor * far_imag).astype(jnp.bfloat16)], 0
        )
        back_real, back_imag = transform(change, tables.at[1], tables.at[0])
        probe_real = probe_ref[0]
        probe_imag = probe_ref[1]
        terms[0] = probe_real * back_real + probe_imag * back_imag
        terms[1] = probe_real * back_imag - probe_imag * back_real
        return carry

    @pl.when(total > 0)
    def _():
        gather(0)
        lax.fori_loop(0, total, step, 0)
        scatter(total - 1)

    if inner:
        return
    peak = jnp.max(probe_ref[0] * probe_ref[0] + probe_ref[1] * probe_ref[1])
    rows = 64

    def finish(wrapped, number, carry):
        place = (pl.ds(pl.multiple_of(number * rows, rows), rows), slice(None))
        beyond = pl.ds(pl.multiple_of(tile_px + number * rows, rows), rows)
        for part in range(2):
            for block in range(width):
                value = gradient[(part, block) + place]
                if wrapped:
                    value = value + gradient[part, block, beyond, :]
                share = value / peak
                if block < blocks:
                    columns = slice(block * LANES, (block + 1) * LANES)
                    main_out[part, place[0], columns] = field[(part, block) + place] + share
                else:
                    columns = slice((block - blocks) * LANES, (block - blocks + 1) * LANES)
                    side_out[part, place[0], columns] = share
        return carry

    lax.fori_loop(0, length // rows, functools.partial(finish, fold), 0)
    lax.fori_loop(length // rows, tile_px // rows, functools.partial(finish, False), 0)
    if fold:
        below_out[...] = jnp.zeros_like(below_out)
    else:
        for block in range(width):
            columns = slice(block * LANES, (block + 1) * LANES)
            below_out[:, :, columns] = gradient[:, block, tile_px:, :] / peak


def patch_call(own_object, probe, measured, corners, fold, margins=()):
    tile_px = own_object.shape[-1]
    length = probe.shape[-1]
    count = measured.shape[0]
    width = tile_px + length
    cosine, sine = fourier_parts(length)
    inner = not margins
    below = (2, 8, LANES) if fold else (2, length, width)
    vmem = pl.BlockSpec(memory_space=pltpu.VMEM)
    anywhere = pl.BlockSpec(memory_space=pl.ANY)
    sums = (2, width // LANES, width, LANES)
    if inner:
        shapes = [sums]
    else:
        shapes = [(2, tile_px, tile_px), (2, tile_px, length), below]
    scratch = [
        pltpu.VMEM(sums, jnp.float32),
        pltpu.VMEM((2, 2 * length, 2 * length), jnp.bfloat16),
        pltpu.VMEM((2 * length, length), jnp.bfloat16),
        pltpu.VMEM((2, length, length), jnp.float32),
        pltpu.SMEM((count + 1,), jnp.int32),
        pltpu.SemaphoreType.DMA((2 * (width // LANES),)),
    ]
    if not inner:
        scratch = [pltpu.VMEM(sums, jnp.float32)] + scratch
    return pl.pallas_call(
        functools.partial(patch_kernel, fold, inner),
        out_shape=[jax.ShapeDtypeStruct(shape, jnp.float32) for shape in shapes],
        in_specs=[pl.BlockSpec(memory_space=pltpu.SMEM), anywhere, vmem, vmem, vmem, vmem]
        + ([] if inner else [anywhere, anywhere, vmem]),
        out_specs=[vmem] * len(shapes),
        scratch_shapes=scratch,
        compiler_params=pltpu.CompilerParams(vmem_limit_bytes=40 * 1024 * 1024),
        cost_estimate=pl.CostEstimate(
            flops=32 * count * length**3, bytes_accessed=16 * tile_px * tile_px, transcendentals=0
        ),
        name="patches_inner" if inner else "patches_outer",
    )(corners, own_object, measured, probe, cosine, sine, *margins)


def fit_scalars(materials_ref, energies, kinds):
    spectra = [
        [materials_ref[(part * energies + energy) * kinds + kind] for kind in range(kinds)]
        for part in range(2)
        for energy in range(energies)
    ]
    gram = [[None] * kinds for _ in range(kinds)]
    for one in range(kinds):
        for other in range(one, kinds):
            total = spectra[0][one] * spectra[0][other]
            for row in spectra[1:]:
                total = total + row[one] * row[other]
            gram[one][other] = total
            gram[other][one] = total
    trace = gram[0][0]
    for one in range(1, kinds):
        trace = trace + gram[one][one]
    return gram, trace


def fit_columns(materials_ref, step_ref, data, spectra, energies, kinds, rate, begin, wide):
    rows = data.shape[2]
    tall = 16 if rows % 16 == 0 else 8
    pairs = [(part, energy) for part in range(2) for energy in range(energies)]

    def chunk(number, carry):
        row = pl.multiple_of(number * tall, tall)
        place = (pl.ds(row, tall), pl.ds(begin, wide))
        target = [None] * kinds
        for part, energy in pairs:
            plane = data[(part, energy) + place]
            for kind in range(kinds):
                term = materials_ref[(part * energies + energy) * kinds + kind] * plane
                target[kind] = term if target[kind] is None else target[kind] + term
        target = [rate * value for value in target]
        current = [jnp.maximum(value, 0.0) for value in target]

        def descend(turn, current):
            following = []
            for one in range(kinds):
                total = target[one]
                for other in range(kinds):
                    total = total + step_ref[one * kinds + other] * current[other]
                following.append(jnp.maximum(total, 0.0))
            return following

        current = lax.fori_loop(1, FIT_STEPS, descend, current)
        for part, energy in pairs:
            total = None
            for kind in range(kinds):
                term = materials_ref[(part * energies + energy) * kinds + kind] * current[kind]
                total = term if total is None else total + term
            spectra[(part, energy) + place] = total
        return carry

    lax.fori_loop(0, rows // tall, chunk, 0)


def exchange_kernel(
    groups,
    tiles,
    materials_ref,
    main_ref,
    side_ref,
    out_ref,
    step_ref,
    margin,
    left,
    data,
    spectra,
    margin_sems,
    send_sems,
    recv_sems,
    own_sems,
):
    mesh_ids = pl.DeviceIdType.MESH
    me = lax.axis_index("energy")
    tile = lax.axis_index("tile")
    after = lax.rem(tile + 1, tiles)
    before = lax.rem(tile + tiles - 1, tiles)
    tile_px = main_ref.shape[-1]
    length = side_ref.shape[-1]
    rows = tile_px // groups
    kinds = materials_ref.shape[0] // (2 * groups)
    offsets = sorted(range(1, groups), key=lambda offset: abs(offset - groups // 2))
    peers = {offset: lax.rem(me + offset, groups) for offset in offsets}

    barrier = pltpu.get_barrier_semaphore()
    for neighbour in (after, before):
        pl.semaphore_signal(barrier, inc=1, device_id=(me, neighbour), device_id_type=mesh_ids)
    for offset in offsets:
        pl.semaphore_signal(
            barrier, inc=1, device_id=(peers[offset], tile), device_id_type=mesh_ids
        )

    gram, trace = fit_scalars(materials_ref, groups, kinds)
    rate = 1.0 / trace
    for one in range(kinds):
        for other in range(kinds):
            unit = 1.0 if one == other else 0.0
            step_ref[one * kinds + other] = unit - rate * gram[one][other]
    pl.semaphore_wait(barrier, groups + 1)

    margin_copy = pltpu.make_async_remote_copy(
        src_ref=side_ref,
        dst_ref=margin,
        send_sem=margin_sems.at[0],
        recv_sem=margin_sems.at[1],
        device_id=(me, after),
        device_id_type=mesh_ids,
    )
    margin_copy.start()

    def rows_of(group):
        return pl.ds(pl.multiple_of(group * rows, rows), rows)

    def outward(block):
        columns = pl.ds(block * LANES, LANES)
        source = left if block * LANES < length else main_ref
        copies = [
            pltpu.make_async_remote_copy(
                src_ref=source.at[:, rows_of(peers[offset]), columns],
                dst_ref=data.at[:, me, :, columns],
                send_sem=send_sems.at[0, block, offset],
                recv_sem=recv_sems.at[0, block, offset],
                device_id=(peers[offset], tile),
                device_id_type=mesh_ids,
            )
            for offset in offsets
        ]
        own = pltpu.make_async_copy(
            source.at[:, rows_of(me), columns], data.at[:, me, :, columns], own_sems.at[0, block]
        )
        return copies, own

    def homeward(block):
        columns = pl.ds(block * LANES, LANES)
        copies = [
            pltpu.make_async_remote_copy(
                src_ref=spectra.at[:, peers[offset], :, columns],
                dst_ref=out_ref.at[:, rows_of(me), columns],
                send_sem=send_sems.at[1, block, offset],
                recv_sem=recv_sems.at[1, block, offset],
                device_id=(peers[offset], tile),
                device_id_type=mesh_ids,
            )
            for offset in offsets
        ]
        own = pltpu.make_async_copy(
            spectra.at[:, me, :, columns], out_ref.at[:, rows_of(me), columns], own_sems.at[1, block]
        )
        return copies, own

    def start(moves):
        for copy in moves[0]:
            copy.start()
        moves[1].start()

    blocks = tile_px // LANES
    early = [block for block in range(blocks) if block * LANES >= length]
    late = [block for block in range(blocks) if block * LANES < length]
    going = {}
    for block in early:
        going[block] = outward(block)
        start(going[block])
    margin_copy.wait()
    for block in late:
        columns = slice(block * LANES, (block + 1) * LANES)
        left[:, :, columns] = main_ref[:, :, columns] + margin[:, :, columns]
    for block in late:
        going[block] = outward(block)
        start(going[block])
    coming = {}
    for block in early + late:
        copies, own = going[block]
        for copy in copies:
            copy.wait_recv()
        own.wait()
        fit_columns(
            materials_ref, step_ref, data, spectra, groups, kinds, rate, block * LANES, LANES
        )
        coming[block] = homeward(block)
        start(coming[block])
    for block in early + late:
        for copy in going[block][0]:
            copy.wait_send()
        copies, own = coming[block]
        own.wait()
        for copy in copies:
            copy.wait()


def exchange_fit(main, side, materials):
    groups = lax.axis_size("energy")
    tiles = lax.axis_size("tile")
    tile_px = main.shape[-1]
    length = side.shape[-1]
    kinds = materials.shape[-1]
    rows = tile_px // groups
    blocks = tile_px // LANES
    vmem = pl.BlockSpec(memory_space=pltpu.VMEM)
    return pl.pallas_call(
        functools.partial(exchange_kernel, groups, tiles),
        out_shape=jax.ShapeDtypeStruct(main.shape, jnp.float32),
        in_specs=[pl.BlockSpec(memory_space=pltpu.SMEM), vmem, vmem],
        out_specs=vmem,
        scratch_shapes=[
            pltpu.SMEM((kinds * kinds,), jnp.float32),
            pltpu.VMEM((2, tile_px, length), jnp.float32),
            pltpu.VMEM((2, tile_px, length), jnp.float32),
            pltpu.VMEM((2, groups, rows, tile_px), jnp.float32),
            pltpu.VMEM((2, groups, rows, tile_px), jnp.float32),
            pltpu.SemaphoreType.DMA((2,)),
            pltpu.SemaphoreType.DMA((2, blocks, groups)),
            pltpu.SemaphoreType.DMA((2, blocks, groups)),
            pltpu.SemaphoreType.DMA((2, blocks)),
        ],
        compiler_params=pltpu.CompilerParams(
            collective_id=0, has_side_effects=True, vmem_limit_bytes=32 * 1024 * 1024
        ),
        name="exchange",
    )(materials.reshape(-1), main, side)


def body(object_tiles, probe_wave, measured, positions, materials):
    own_object = object_tiles[0, :, 0]
    tile_px = own_object.shape[-1]
    length = probe_wave.shape[-1]
    tile_count = lax.axis_size("tile")
    row_step = TILE_COLS % tile_count
    fold = row_step == 0
    right_strip = shifted(own_object[:, :, :length], "tile", -1)
    if fold:
        lower_strip = jnp.zeros((2, 8, LANES), jnp.float32)
    else:
        widened = jnp.concatenate([own_object[:, :length], right_strip[:, :length]], 2)
        lower_strip = shifted(widened, "tile", -row_step)
    shared = (own_object, probe_wave[0], measured[0, 0], positions[0], fold)
    (begun,) = patch_call(*shared)
    main, side, below = patch_call(*shared, margins=(right_strip, lower_strip, begun))
    if not fold:
        from_above = shifted(below, "tile", row_step)
        main = main.at[:, :length, :].add(from_above[:, :, :tile_px])
        side = side.at[:, :length, :].add(from_above[:, :, tile_px:])
    fitted = exchange_fit(main, side, materials)
    return fitted.reshape(1, 2, 1, tile_px, tile_px)


def solution(mesh):
    in_specs = (
        P("energy", None, "tile", None, None),
        P("energy", None, None, None),
        P("energy", "tile", None, None, None),
        P("tile", None, None),
        P(),
    )
    out_specs = P("energy", None, "tile", None, None)
    return jax.shard_map(body, mesh=mesh, in_specs=in_specs, out_specs=out_specs, check_vma=False)
```

```python
import functools
import math

import jax
import jax.numpy as jnp
import numpy as np
from jax import lax
from jax.experimental import pallas as pl
from jax.experimental.pallas import tpu as pltpu
from jax.sharding import PartitionSpec as P

TILE_COLS = 4
FIT_STEPS = 10
LANES = 128


amplitude_floor = 0.5


def shifted(value, axis, steps):
    count = lax.axis_size(axis)
    pairs = [(source, (source + steps) % count) for source in range(count)]
    return lax.ppermute(value, axis, pairs)


def fourier_parts(length):
    counter = np.arange(length, dtype=np.int64)
    angles = 2.0 * math.pi / length * (counter[:, None] * counter[None, :] % length)
    return (
        jnp.asarray(np.cos(angles), jnp.float32).astype(jnp.bfloat16),
        jnp.asarray(np.sin(angles), jnp.float32).astype(jnp.bfloat16),
    )


def joined(top_left, top_right, bottom_left, bottom_right):
    return jnp.concatenate(
        [
            jnp.concatenate([top_left, top_right], 1),
            jnp.concatenate([bottom_left, bottom_right], 1),
        ],
        0,
    )


def transform(stacked, left_ref, right_ref):
    length = stacked.shape[0] // 2
    inner = jnp.dot(left_ref[...], stacked, preferred_element_type=jnp.float32)
    inner = inner.astype(jnp.bfloat16)
    beside = jnp.concatenate([inner[:length], inner[length:]], 1)
    outer = jnp.dot(beside, right_ref[...], preferred_element_type=jnp.float32) * (1.0 / length)
    return outer[:, :length], outer[:, length:]


def window(ref, part, row, block, shift, length):
    lane = lax.broadcasted_iota(jnp.int32, (length, LANES), 1)
    back = lax.rem(LANES - shift, LANES)
    tiles = [
        pltpu.roll(ref[part, block + at, pl.ds(row, length), :], back, 1)
        for at in range(length // LANES + 1)
    ]
    keep = lane < LANES - shift
    return jnp.concatenate(
        [jnp.where(keep, one, other) for one, other in zip(tiles[:-1], tiles[1:])], 1
    )


def add_window(ref, part, row, block, shift, term):
    length = term.shape[0]
    lane = lax.broadcasted_iota(jnp.int32, (length, LANES), 1)
    tiles = [pltpu.roll(term[:, at : at + LANES], shift, 1) for at in range(0, length, LANES)]
    keep = lane >= shift
    zero = jnp.zeros_like(tiles[0])
    for at, (one, other) in enumerate(zip(tiles + [zero], [zero] + tiles)):
        place = (part, block + at, pl.ds(row, length), slice(None))
        ref[place] = ref[place] + jnp.where(keep, one, other)


def patch_kernel(fold, inner, *refs):
    corners_ref, object_ref, measured_ref, probe_ref, cosine_ref, sine_ref = refs[:6]
    if inner:
        (gradient,) = refs[6:7]
        right_ref = lower_ref = None
        rest = refs[7:]
    else:
        right_ref, lower_ref, begun_ref, main_out, side_out, below_out = refs[6:12]
        gradient, *rest = refs[12:]
    field, tables, wave, change, terms, order, sems = rest
    tile_px = object_ref.shape[-1]
    length = probe_ref.shape[-1]
    count = measured_ref.shape[0]
    blocks = tile_px // LANES
    width = blocks + length // LANES
    top = pl.ds(0, tile_px)
    bottom = pl.ds(tile_px, length)
    moves = []
    for block in range(blocks if inner else width):
        ref, at = (object_ref, block) if block < blocks else (right_ref, block - blocks)
        columns = pl.ds(at * LANES, LANES)
        moves.append((ref.at[:, :, columns], field.at[:, block, top, :]))
        if fold:
            source = ref.at[:, pl.ds(0, length), columns]
        elif not inner:
            source = lower_ref.at[:, :, pl.ds(block * LANES, LANES)]
        else:
            continue
        moves.append((source, field.at[:, block, bottom, :]))
    copies = [
        pltpu.make_async_copy(source, target, sems.at[number])
        for number, (source, target) in enumerate(moves)
    ]
    for copy in copies:
        copy.start()
    cosine = cosine_ref[...]
    sine = sine_ref[...]
    tables[0] = joined(cosine, sine, -sine, cosine)
    tables[1] = joined(cosine, -sine, sine, cosine)
    if inner:
        gradient[...] = jnp.zeros_like(gradient)
    else:
        gradient[...] = begun_ref[...]
    terms[...] = jnp.zeros_like(terms)

    limit = tile_px - length

    def choose(number, found):
        order[found] = number
        within = corners_ref[number, 1] <= limit
        if not fold:
            within = jnp.logical_and(within, corners_ref[number, 0] <= limit)
        return found + jnp.where(within, int(inner), 1 - int(inner))

    total = lax.fori_loop(0, count, choose, 0)
    for copy in copies:
        copy.wait()

    def corner(turn):
        number = order[turn]
        row = corners_ref[number, 0]
        col = corners_ref[number, 1]
        block = col // LANES
        return number, row, block, col - block * LANES

    def gather(turn):
        _, row, block, shift = corner(turn)
        piece_real = window(field, 0, row, block, shift, length)
        piece_imag = window(field, 1, row, block, shift, length)
        probe_real = probe_ref[0]
        probe_imag = probe_ref[1]
        exit_real = probe_real * piece_real - probe_imag * piece_imag
        exit_imag = probe_real * piece_imag + probe_imag * piece_real
        wave[:length, :] = exit_real.astype(jnp.bfloat16)
        wave[length:, :] = exit_imag.astype(jnp.bfloat16)

    def scatter(turn):
        _, row, block, shift = corner(turn)
        add_window(gradient, 0, row, block, shift, terms[0])
        add_window(gradient, 1, row, block, shift, terms[1])

    def outward(turn):
        far_real, far_imag = transform(wave[...], tables.at[0], tables.at[1])
        square = far_real * far_real + far_imag * far_imag
        scale = lax.rsqrt(jnp.maximum(square, amplitude_floor * amplitude_floor))
        factor = measured_ref[order[turn]].astype(jnp.float32) * scale - 1.0
        return (factor * far_real).astype(jnp.bfloat16), (factor * far_imag).astype(jnp.bfloat16)

    def keep(parts):
        change[:length, :] = parts[0]
        change[length:, :] = parts[1]

    def homeward():
        back_real, back_imag = transform(change[...], tables.at[1], tables.at[0])
        probe_real = probe_ref[0]
        probe_imag = probe_ref[1]
        return (
            probe_real * back_real + probe_imag * back_imag,
            probe_real * back_imag - probe_imag * back_real,
        )

    def step(turn, carry):
        scatter(jnp.maximum(turn - 1, 0))
        parts = outward(turn + 1)
        back = homeward()
        keep(parts)
        gather(jnp.minimum(turn + 2, total - 1))
        terms[0] = back[0]
        terms[1] = back[1]
        return carry

    @pl.when(total > 0)
    def _():
        gather(0)
        keep(outward(0))
        gather(jnp.minimum(1, total - 1))
        lax.fori_loop(0, total - 1, step, 0)
        scatter(jnp.maximum(total - 2, 0))
        back = homeward()
        terms[0] = back[0]
        terms[1] = back[1]
        scatter(total - 1)

    if inner:
        return
    peak = jnp.max(probe_ref[0] * probe_ref[0] + probe_ref[1] * probe_ref[1])
    rows = 64

    def finish(wrapped, number, carry):
        place = (pl.ds(pl.multiple_of(number * rows, rows), rows), slice(None))
        beyond = pl.ds(pl.multiple_of(tile_px + number * rows, rows), rows)
        for part in range(2):
            for block in range(width):
                value = gradient[(part, block) + place]
                if wrapped:
                    value = value + gradient[part, block, beyond, :]
                share = value / peak
                if block < blocks:
                    columns = slice(block * LANES, (block + 1) * LANES)
                    main_out[part, place[0], columns] = field[(part, block) + place] + share
                else:
                    columns = slice((block - blocks) * LANES, (block - blocks + 1) * LANES)
                    side_out[part, place[0], columns] = share
        return carry

    lax.fori_loop(0, length // rows, functools.partial(finish, fold), 0)
    lax.fori_loop(length // rows, tile_px // rows, functools.partial(finish, False), 0)
    if fold:
        below_out[...] = jnp.zeros_like(below_out)
    else:
        for block in range(width):
            columns = slice(block * LANES, (block + 1) * LANES)
            below_out[:, :, columns] = gradient[:, block, tile_px:, :] / peak


def patch_call(own_object, probe, measured, corners, fold, margins=()):
    tile_px = own_object.shape[-1]
    length = probe.shape[-1]
    count = measured.shape[0]
    width = tile_px + length
    cosine, sine = fourier_parts(length)
    inner = not margins
    below = (2, 8, LANES) if fold else (2, length, width)
    vmem = pl.BlockSpec(memory_space=pltpu.VMEM)
    anywhere = pl.BlockSpec(memory_space=pl.ANY)
    sums = (2, width // LANES, width, LANES)
    if inner:
        shapes = [sums]
    else:
        shapes = [(2, tile_px, tile_px), (2, tile_px, length), below]
    scratch = [
        pltpu.VMEM(sums, jnp.float32),
        pltpu.VMEM((2, 2 * length, 2 * length), jnp.bfloat16),
        pltpu.VMEM((2 * length, length), jnp.bfloat16),
        pltpu.VMEM((2 * length, length), jnp.bfloat16),
        pltpu.VMEM((2, length, length), jnp.float32),
        pltpu.SMEM((count + 1,), jnp.int32),
        pltpu.SemaphoreType.DMA((2 * (width // LANES),)),
    ]
    if not inner:
        scratch = [pltpu.VMEM(sums, jnp.float32)] + scratch
    return pl.pallas_call(
        functools.partial(patch_kernel, fold, inner),
        out_shape=[jax.ShapeDtypeStruct(shape, jnp.float32) for shape in shapes],
        in_specs=[pl.BlockSpec(memory_space=pltpu.SMEM), anywhere, vmem, vmem, vmem, vmem]
        + ([] if inner else [anywhere, anywhere, vmem]),
        out_specs=[vmem] * len(shapes),
        scratch_shapes=scratch,
        compiler_params=pltpu.CompilerParams(vmem_limit_bytes=40 * 1024 * 1024),
        cost_estimate=pl.CostEstimate(
            flops=32 * count * length**3, bytes_accessed=16 * tile_px * tile_px, transcendentals=0
        ),
        name="patches_inner" if inner else "patches_outer",
    )(corners, own_object, measured, probe, cosine, sine, *margins)


def fit_scalars(materials_ref, energies, kinds):
    spectra = [
        [materials_ref[(part * energies + energy) * kinds + kind] for kind in range(kinds)]
        for part in range(2)
        for energy in range(energies)
    ]
    gram = [[None] * kinds for _ in range(kinds)]
    for one in range(kinds):
        for other in range(one, kinds):
            total = spectra[0][one] * spectra[0][other]
            for row in spectra[1:]:
                total = total + row[one] * row[other]
            gram[one][other] = total
            gram[other][one] = total
    trace = gram[0][0]
    for one in range(1, kinds):
        trace = trace + gram[one][one]
    return gram, trace


def fit_columns(materials_ref, step_ref, data, spectra, energies, kinds, rate, begin, wide):
    rows = data.shape[2]
    tall = 16 if rows % 16 == 0 else 8
    pairs = [(part, energy) for part in range(2) for energy in range(energies)]

    def chunk(number, carry):
        row = pl.multiple_of(number * tall, tall)
        place = (pl.ds(row, tall), pl.ds(begin, wide))
        target = [None] * kinds
        for part, energy in pairs:
            plane = data[(part, energy) + place]
            for kind in range(kinds):
                term = materials_ref[(part * energies + energy) * kinds + kind] * plane
                target[kind] = term if target[kind] is None else target[kind] + term
        target = [rate * value for value in target]
        current = [jnp.maximum(value, 0.0) for value in target]

        def descend(turn, current):
            following = []
            for one in range(kinds):
                total = target[one]
                for other in range(kinds):
                    total = total + step_ref[one * kinds + other] * current[other]
                following.append(jnp.maximum(total, 0.0))
            return following

        current = lax.fori_loop(1, FIT_STEPS, descend, current)
        for part, energy in pairs:
            total = None
            for kind in range(kinds):
                term = materials_ref[(part * energies + energy) * kinds + kind] * current[kind]
                total = term if total is None else total + term
            spectra[(part, energy) + place] = total
        return carry

    lax.fori_loop(0, rows // tall, chunk, 0)


def exchange_kernel(
    groups,
    tiles,
    materials_ref,
    main_ref,
    side_ref,
    out_ref,
    step_ref,
    margin,
    left,
    data,
    spectra,
    margin_sems,
    send_sems,
    recv_sems,
    own_sems,
):
    mesh_ids = pl.DeviceIdType.MESH
    me = lax.axis_index("energy")
    tile = lax.axis_index("tile")
    after = lax.rem(tile + 1, tiles)
    before = lax.rem(tile + tiles - 1, tiles)
    tile_px = main_ref.shape[-1]
    length = side_ref.shape[-1]
    rows = tile_px // groups
    kinds = materials_ref.shape[0] // (2 * groups)
    offsets = sorted(range(1, groups), key=lambda offset: abs(offset - groups // 2))
    peers = {offset: lax.rem(me + offset, groups) for offset in offsets}

    barrier = pltpu.get_barrier_semaphore()
    for neighbour in (after, before):
        pl.semaphore_signal(barrier, inc=1, device_id=(me, neighbour), device_id_type=mesh_ids)
    for offset in offsets:
        pl.semaphore_signal(
            barrier, inc=1, device_id=(peers[offset], tile), device_id_type=mesh_ids
        )

    pl.semaphore_wait(barrier, groups + 1)

    margin_copy = pltpu.make_async_remote_copy(
        src_ref=side_ref,
        dst_ref=margin,
        send_sem=margin_sems.at[0],
        recv_sem=margin_sems.at[1],
        device_id=(me, after),
        device_id_type=mesh_ids,
    )
    margin_copy.start()

    def rows_of(group):
        return pl.ds(pl.multiple_of(group * rows, rows), rows)

    def outward(block):
        columns = pl.ds(block * LANES, LANES)
        source = left if block * LANES < length else main_ref
        copies = [
            pltpu.make_async_remote_copy(
                src_ref=source.at[:, rows_of(peers[offset]), columns],
                dst_ref=data.at[:, me, :, columns],
                send_sem=send_sems.at[0, block, offset],
                recv_sem=recv_sems.at[0, block, offset],
                device_id=(peers[offset], tile),
                device_id_type=mesh_ids,
            )
            for offset in offsets
        ]
        own = pltpu.make_async_copy(
            source.at[:, rows_of(me), columns], data.at[:, me, :, columns], own_sems.at[0, block]
        )
        return copies, own

    def homeward(block):
        columns = pl.ds(block * LANES, LANES)
        copies = [
            pltpu.make_async_remote_copy(
                src_ref=spectra.at[:, peers[offset], :, columns],
                dst_ref=out_ref.at[:, rows_of(me), columns],
                send_sem=send_sems.at[1, block, offset],
                recv_sem=recv_sems.at[1, block, offset],
                device_id=(peers[offset], tile),
                device_id_type=mesh_ids,
            )
            for offset in offsets
        ]
        own = pltpu.make_async_copy(
            spectra.at[:, me, :, columns], out_ref.at[:, rows_of(me), columns], own_sems.at[1, block]
        )
        return copies, own

    def start(moves):
        for copy in moves[0]:
            copy.start()
        moves[1].start()

    blocks = tile_px // LANES
    early = [block for block in range(blocks) if block * LANES >= length]
    late = [block for block in range(blocks) if block * LANES < length]
    going = {}
    for block in early:
        going[block] = outward(block)
        start(going[block])

    gram, trace = fit_scalars(materials_ref, groups, kinds)
    rate = 1.0 / trace
    for one in range(kinds):
        for other in range(kinds):
            unit = 1.0 if one == other else 0.0
            step_ref[one * kinds + other] = unit - rate * gram[one][other]
    margin_copy.wait()
    for block in late:
        columns = slice(block * LANES, (block + 1) * LANES)
        left[:, :, columns] = main_ref[:, :, columns] + margin[:, :, columns]
    for block in late:
        going[block] = outward(block)
        start(going[block])
    coming = {}
    for block in early + late:
        copies, own = going[block]
        for copy in copies:
            copy.wait_recv()
        own.wait()
        fit_columns(
            materials_ref, step_ref, data, spectra, groups, kinds, rate, block * LANES, LANES
        )
        coming[block] = homeward(block)
        start(coming[block])
    for block in early + late:
        for copy in going[block][0]:
            copy.wait_send()
        copies, own = coming[block]
        own.wait()
        for copy in copies:
            copy.wait()


def exchange_fit(main, side, materials):
    groups = lax.axis_size("energy")
    tiles = lax.axis_size("tile")
    tile_px = main.shape[-1]
    length = side.shape[-1]
    kinds = materials.shape[-1]
    rows = tile_px // groups
    blocks = tile_px // LANES
    vmem = pl.BlockSpec(memory_space=pltpu.VMEM)
    return pl.pallas_call(
        functools.partial(exchange_kernel, groups, tiles),
        out_shape=jax.ShapeDtypeStruct(main.shape, jnp.float32),
        in_specs=[pl.BlockSpec(memory_space=pltpu.SMEM), vmem, vmem],
        out_specs=vmem,
        scratch_shapes=[
            pltpu.SMEM((kinds * kinds,), jnp.float32),
            pltpu.VMEM((2, tile_px, length), jnp.float32),
            pltpu.VMEM((2, tile_px, length), jnp.float32),
            pltpu.VMEM((2, groups, rows, tile_px), jnp.float32),
            pltpu.VMEM((2, groups, rows, tile_px), jnp.float32),
            pltpu.SemaphoreType.DMA((2,)),
            pltpu.SemaphoreType.DMA((2, blocks, groups)),
            pltpu.SemaphoreType.DMA((2, blocks, groups)),
            pltpu.SemaphoreType.DMA((2, blocks)),
        ],
        compiler_params=pltpu.CompilerParams(
            collective_id=0, has_side_effects=True, vmem_limit_bytes=32 * 1024 * 1024
        ),
        name="exchange",
    )(materials.reshape(-1), main, side)


def body(object_tiles, probe_wave, measured, positions, materials):
    own_object = object_tiles[0, :, 0]
    tile_px = own_object.shape[-1]
    length = probe_wave.shape[-1]
    tile_count = lax.axis_size("tile")
    row_step = TILE_COLS % tile_count
    fold = row_step == 0
    right_strip = shifted(own_object[:, :, :length], "tile", -1)
    if fold:
        lower_strip = jnp.zeros((2, 8, LANES), jnp.float32)
    else:
        widened = jnp.concatenate([own_object[:, :length], right_strip[:, :length]], 2)
        lower_strip = shifted(widened, "tile", -row_step)
    shared = (own_object, probe_wave[0], measured[0, 0], positions[0], fold)
    (begun,) = patch_call(*shared)
    main, side, below = patch_call(*shared, margins=(right_strip, lower_strip, begun))
    if not fold:
        from_above = shifted(below, "tile", row_step)
        main = main.at[:, :length, :].add(from_above[:, :, :tile_px])
        side = side.at[:, :length, :].add(from_above[:, :, tile_px:])
    fitted = exchange_fit(main, side, materials)
    return fitted.reshape(1, 2, 1, tile_px, tile_px)


def solution(mesh):
    in_specs = (
        P("energy", None, "tile", None, None),
        P("energy", None, None, None),
        P("energy", "tile", None, None, None),
        P("tile", None, None),
        P(),
    )
    out_specs = P("energy", None, "tile", None, None)
    return jax.shard_map(body, mesh=mesh, in_specs=in_specs, out_specs=out_specs, check_vma=False)
```

```python
import functools
import math

import jax
import jax.numpy as jnp
import numpy as np
from jax import lax
from jax.experimental import pallas as pl
from jax.experimental.pallas import tpu as pltpu
from jax.sharding import PartitionSpec as P

TILE_COLS = 4
FIT_STEPS = 10
LANES = 128


amplitude_floor = 0.5


def shifted(value, axis, steps):
    count = lax.axis_size(axis)
    pairs = [(source, (source + steps) % count) for source in range(count)]
    return lax.ppermute(value, axis, pairs)


def fourier_parts(length):
    counter = np.arange(length, dtype=np.int64)
    angles = 2.0 * math.pi / length * (counter[:, None] * counter[None, :] % length)
    return jnp.asarray(
        np.stack([np.cos(angles), np.sin(angles)]).astype(np.float32).astype(jnp.bfloat16)
    )


def joined(top_left, top_right, bottom_left, bottom_right):
    return jnp.concatenate(
        [
            jnp.concatenate([top_left, top_right], 1),
            jnp.concatenate([bottom_left, bottom_right], 1),
        ],
        0,
    )


def transform(stacked, left_ref, right_ref):
    length = stacked.shape[0] // 2
    inner = jnp.dot(left_ref[...], stacked, preferred_element_type=jnp.float32)
    inner = inner.astype(jnp.bfloat16)
    beside = jnp.concatenate([inner[:length], inner[length:]], 1)
    outer = jnp.dot(beside, right_ref[...], preferred_element_type=jnp.float32) * (1.0 / length)
    return outer[:, :length], outer[:, length:]


def window(ref, part, row, block, shift, length):
    lane = lax.broadcasted_iota(jnp.int32, (length, LANES), 1)
    back = lax.rem(LANES - shift, LANES)
    tiles = [
        pltpu.roll(ref[part, block + at, pl.ds(row, length), :], back, 1)
        for at in range(length // LANES + 1)
    ]
    keep = lane < LANES - shift
    return jnp.concatenate(
        [jnp.where(keep, one, other) for one, other in zip(tiles[:-1], tiles[1:])], 1
    )


def add_window(ref, part, row, block, shift, term):
    length = term.shape[0]
    lane = lax.broadcasted_iota(jnp.int32, (length, LANES), 1)
    tiles = [pltpu.roll(term[:, at : at + LANES], shift, 1) for at in range(0, length, LANES)]
    keep = lane >= shift
    zero = jnp.zeros_like(tiles[0])
    for at, (one, other) in enumerate(zip(tiles + [zero], [zero] + tiles)):
        place = (part, block + at, pl.ds(row, length), slice(None))
        ref[place] = ref[place] + jnp.where(keep, one, other)


def patch_kernel(fold, inner, *refs):
    corners_ref, object_ref, measured_ref, probe_ref, fourier_ref = refs[:5]
    if inner:
        (gradient,) = refs[5:6]
        right_ref = lower_ref = None
        rest = refs[6:]
    else:
        right_ref, lower_ref, begun_ref, main_out, side_out, below_out = refs[5:11]
        gradient, *rest = refs[11:]
    field, tables, wave, change, terms, order, sems = rest
    tile_px = object_ref.shape[-1]
    length = probe_ref.shape[-1]
    count = measured_ref.shape[0]
    blocks = tile_px // LANES
    width = blocks + length // LANES
    top = pl.ds(0, tile_px)
    bottom = pl.ds(tile_px, length)
    moves = []
    for block in range(blocks if inner else width):
        ref, at = (object_ref, block) if block < blocks else (right_ref, block - blocks)
        columns = pl.ds(at * LANES, LANES)
        moves.append((ref.at[:, :, columns], field.at[:, block, top, :]))
        if fold:
            source = ref.at[:, pl.ds(0, length), columns]
        elif not inner:
            source = lower_ref.at[:, :, pl.ds(block * LANES, LANES)]
        else:
            continue
        moves.append((source, field.at[:, block, bottom, :]))
    copies = [
        pltpu.make_async_copy(source, target, sems.at[number])
        for number, (source, target) in enumerate(moves)
    ]
    for copy in copies:
        copy.start()
    cosine = fourier_ref[0]
    sine = fourier_ref[1]
    tables[0] = joined(cosine, sine, -sine, cosine)
    tables[1] = joined(cosine, -sine, sine, cosine)
    if inner:
        gradient[...] = jnp.zeros_like(gradient)
    else:
        gradient[...] = begun_ref[...]
    terms[...] = jnp.zeros_like(terms)

    limit = tile_px - length

    def choose(number, found):
        order[found] = number
        within = corners_ref[number, 1] <= limit
        if not fold:
            within = jnp.logical_and(within, corners_ref[number, 0] <= limit)
        return found + jnp.where(within, int(inner), 1 - int(inner))

    total = lax.fori_loop(0, count, choose, 0)
    for copy in copies:
        copy.wait()

    def corner(turn):
        number = order[turn]
        row = corners_ref[number, 0]
        col = corners_ref[number, 1]
        block = col // LANES
        return number, row, block, col - block * LANES

    def gather(turn):
        _, row, block, shift = corner(turn)
        piece_real = window(field, 0, row, block, shift, length)
        piece_imag = window(field, 1, row, block, shift, length)
        probe_real = probe_ref[0]
        probe_imag = probe_ref[1]
        exit_real = probe_real * piece_real - probe_imag * piece_imag
        exit_imag = probe_real * piece_imag + probe_imag * piece_real
        wave[:length, :] = exit_real.astype(jnp.bfloat16)
        wave[length:, :] = exit_imag.astype(jnp.bfloat16)

    def scatter(turn):
        _, row, block, shift = corner(turn)
        add_window(gradient, 0, row, block, shift, terms[0])
        add_window(gradient, 1, row, block, shift, terms[1])

    def outward(turn):
        far_real, far_imag = transform(wave[...], tables.at[0], tables.at[1])
        square = far_real * far_real + far_imag * far_imag
        scale = lax.rsqrt(jnp.maximum(square, amplitude_floor * amplitude_floor))
        factor = measured_ref[order[turn]].astype(jnp.float32) * scale - 1.0
        return (factor * far_real).astype(jnp.bfloat16), (factor * far_imag).astype(jnp.bfloat16)

    def keep(parts):
        change[:length, :] = parts[0]
        change[length:, :] = parts[1]

    def homeward():
        back_real, back_imag = transform(change[...], tables.at[1], tables.at[0])
        probe_real = probe_ref[0]
        probe_imag = probe_ref[1]
        return (
            probe_real * back_real + probe_imag * back_imag,
            probe_real * back_imag - probe_imag * back_real,
        )

    def step(turn, carry):
        scatter(jnp.maximum(turn - 1, 0))
        parts = outward(turn + 1)
        back = homeward()
        keep(parts)
        gather(jnp.minimum(turn + 2, total - 1))
        terms[0] = back[0]
        terms[1] = back[1]
        return carry

    @pl.when(total > 0)
    def _():
        gather(0)
        keep(outward(0))
        gather(jnp.minimum(1, total - 1))
        lax.fori_loop(0, total - 1, step, 0)
        scatter(jnp.maximum(total - 2, 0))
        back = homeward()
        terms[0] = back[0]
        terms[1] = back[1]
        scatter(total - 1)

    if inner:
        return
    peak = jnp.max(probe_ref[0] * probe_ref[0] + probe_ref[1] * probe_ref[1])
    rows = 64

    def finish(wrapped, number, carry):
        place = (pl.ds(pl.multiple_of(number * rows, rows), rows), slice(None))
        beyond = pl.ds(pl.multiple_of(tile_px + number * rows, rows), rows)
        for part in range(2):
            for block in range(width):
                value = gradient[(part, block) + place]
                if wrapped:
                    value = value + gradient[part, block, beyond, :]
                share = value / peak
                if block < blocks:
                    columns = slice(block * LANES, (block + 1) * LANES)
                    main_out[part, place[0], columns] = field[(part, block) + place] + share
                else:
                    columns = slice((block - blocks) * LANES, (block - blocks + 1) * LANES)
                    side_out[part, place[0], columns] = share
        return carry

    lax.fori_loop(0, length // rows, functools.partial(finish, fold), 0)
    lax.fori_loop(length // rows, tile_px // rows, functools.partial(finish, False), 0)
    if fold:
        below_out[...] = jnp.zeros_like(below_out)
    else:
        for block in range(width):
            columns = slice(block * LANES, (block + 1) * LANES)
            below_out[:, :, columns] = gradient[:, block, tile_px:, :] / peak


def patch_call(own_object, probe, measured, corners, fold, margins=()):
    tile_px = own_object.shape[-1]
    length = probe.shape[-1]
    count = measured.shape[0]
    width = tile_px + length
    inner = not margins
    below = (2, 8, LANES) if fold else (2, length, width)
    vmem = pl.BlockSpec(memory_space=pltpu.VMEM)
    anywhere = pl.BlockSpec(memory_space=pl.ANY)
    sums = (2, width // LANES, width, LANES)
    if inner:
        shapes = [sums]
    else:
        shapes = [(2, tile_px, tile_px), (2, tile_px, length), below]
    scratch = [
        pltpu.VMEM(sums, jnp.float32),
        pltpu.VMEM((2, 2 * length, 2 * length), jnp.bfloat16),
        pltpu.VMEM((2 * length, length), jnp.bfloat16),
        pltpu.VMEM((2 * length, length), jnp.bfloat16),
        pltpu.VMEM((2, length, length), jnp.float32),
        pltpu.SMEM((count + 1,), jnp.int32),
        pltpu.SemaphoreType.DMA((2 * (width // LANES),)),
    ]
    if not inner:
        scratch = [pltpu.VMEM(sums, jnp.float32)] + scratch
    return pl.pallas_call(
        functools.partial(patch_kernel, fold, inner),
        out_shape=[jax.ShapeDtypeStruct(shape, jnp.float32) for shape in shapes],
        in_specs=[pl.BlockSpec(memory_space=pltpu.SMEM), anywhere, vmem, vmem, vmem]
        + ([] if inner else [anywhere, anywhere, vmem]),
        out_specs=[vmem] * len(shapes),
        scratch_shapes=scratch,
        compiler_params=pltpu.CompilerParams(vmem_limit_bytes=40 * 1024 * 1024),
        cost_estimate=pl.CostEstimate(
            flops=32 * count * length**3, bytes_accessed=16 * tile_px * tile_px, transcendentals=0
        ),
        name="patches_inner" if inner else "patches_outer",
    )(corners, own_object, measured, probe, fourier_parts(length), *margins)


def fit_scalars(materials_ref, energies, kinds):
    spectra = [
        [materials_ref[(part * energies + energy) * kinds + kind] for kind in range(kinds)]
        for part in range(2)
        for energy in range(energies)
    ]
    gram = [[None] * kinds for _ in range(kinds)]
    for one in range(kinds):
        for other in range(one, kinds):
            total = spectra[0][one] * spectra[0][other]
            for row in spectra[1:]:
                total = total + row[one] * row[other]
            gram[one][other] = total
            gram[other][one] = total
    trace = gram[0][0]
    for one in range(1, kinds):
        trace = trace + gram[one][one]
    return gram, trace


def fit_columns(materials_ref, step_ref, data, spectra, energies, kinds, rate, begin, wide):
    rows = data.shape[2]
    tall = 16 if rows % 16 == 0 else 8
    pairs = [(part, energy) for part in range(2) for energy in range(energies)]

    def chunk(number, carry):
        row = pl.multiple_of(number * tall, tall)
        place = (pl.ds(row, tall), pl.ds(begin, wide))
        target = [None] * kinds
        for part, energy in pairs:
            plane = data[(part, energy) + place]
            for kind in range(kinds):
                term = materials_ref[(part * energies + energy) * kinds + kind] * plane
                target[kind] = term if target[kind] is None else target[kind] + term
        target = [rate * value for value in target]
        current = [jnp.maximum(value, 0.0) for value in target]

        def descend(turn, current):
            following = []
            for one in range(kinds):
                total = target[one]
                for other in range(kinds):
                    total = total + step_ref[one * kinds + other] * current[other]
                following.append(jnp.maximum(total, 0.0))
            return following

        current = lax.fori_loop(1, FIT_STEPS, descend, current)
        for part, energy in pairs:
            total = None
            for kind in range(kinds):
                term = materials_ref[(part * energies + energy) * kinds + kind] * current[kind]
                total = term if total is None else total + term
            spectra[(part, energy) + place] = total
        return carry

    lax.fori_loop(0, rows // tall, chunk, 0)


def exchange_kernel(
    groups,
    tiles,
    materials_ref,
    main_ref,
    side_ref,
    out_ref,
    step_ref,
    margin,
    left,
    data,
    spectra,
    margin_sems,
    send_sems,
    recv_sems,
    own_sems,
):
    mesh_ids = pl.DeviceIdType.MESH
    me = lax.axis_index("energy")
    tile = lax.axis_index("tile")
    after = lax.rem(tile + 1, tiles)
    before = lax.rem(tile + tiles - 1, tiles)
    tile_px = main_ref.shape[-1]
    length = side_ref.shape[-1]
    rows = tile_px // groups
    kinds = materials_ref.shape[0] // (2 * groups)
    offsets = sorted(range(1, groups), key=lambda offset: abs(offset - groups // 2))
    peers = {offset: lax.rem(me + offset, groups) for offset in offsets}

    barrier = pltpu.get_barrier_semaphore()
    for neighbour in (after, before):
        pl.semaphore_signal(barrier, inc=1, device_id=(me, neighbour), device_id_type=mesh_ids)
    for offset in offsets:
        pl.semaphore_signal(
            barrier, inc=1, device_id=(peers[offset], tile), device_id_type=mesh_ids
        )

    pl.semaphore_wait(barrier, groups + 1)

    margin_copy = pltpu.make_async_remote_copy(
        src_ref=side_ref,
        dst_ref=margin,
        send_sem=margin_sems.at[0],
        recv_sem=margin_sems.at[1],
        device_id=(me, after),
        device_id_type=mesh_ids,
    )
    margin_copy.start()

    def rows_of(group):
        return pl.ds(pl.multiple_of(group * rows, rows), rows)

    def outward(block):
        columns = pl.ds(block * LANES, LANES)
        source = left if block * LANES < length else main_ref
        copies = [
            pltpu.make_async_remote_copy(
                src_ref=source.at[:, rows_of(peers[offset]), columns],
                dst_ref=data.at[:, me, :, columns],
                send_sem=send_sems.at[0, block, offset],
                recv_sem=recv_sems.at[0, block, offset],
                device_id=(peers[offset], tile),
                device_id_type=mesh_ids,
            )
            for offset in offsets
        ]
        own = pltpu.make_async_copy(
            source.at[:, rows_of(me), columns], data.at[:, me, :, columns], own_sems.at[0, block]
        )
        return copies, own

    def homeward(block):
        columns = pl.ds(block * LANES, LANES)
        copies = [
            pltpu.make_async_remote_copy(
                src_ref=spectra.at[:, peers[offset], :, columns],
                dst_ref=out_ref.at[:, rows_of(me), columns],
                send_sem=send_sems.at[1, block, offset],
                recv_sem=recv_sems.at[1, block, offset],
                device_id=(peers[offset], tile),
                device_id_type=mesh_ids,
            )
            for offset in offsets
        ]
        own = pltpu.make_async_copy(
            spectra.at[:, me, :, columns], out_ref.at[:, rows_of(me), columns], own_sems.at[1, block]
        )
        return copies, own

    def start(moves):
        for copy in moves[0]:
            copy.start()
        moves[1].start()

    blocks = tile_px // LANES
    early = [block for block in range(blocks) if block * LANES >= length]
    late = [block for block in range(blocks) if block * LANES < length]
    going = {}
    for block in early:
        going[block] = outward(block)
        start(going[block])

    gram, trace = fit_scalars(materials_ref, groups, kinds)
    rate = 1.0 / trace
    for one in range(kinds):
        for other in range(kinds):
            unit = 1.0 if one == other else 0.0
            step_ref[one * kinds + other] = unit - rate * gram[one][other]
    margin_copy.wait()
    for block in late:
        columns = slice(block * LANES, (block + 1) * LANES)
        left[:, :, columns] = main_ref[:, :, columns] + margin[:, :, columns]
    for block in late:
        going[block] = outward(block)
        start(going[block])
    coming = {}
    for block in early + late:
        copies, own = going[block]
        for copy in copies:
            copy.wait_recv()
        own.wait()
        fit_columns(
            materials_ref, step_ref, data, spectra, groups, kinds, rate, block * LANES, LANES
        )
        coming[block] = homeward(block)
        start(coming[block])
    for block in early + late:
        for copy in going[block][0]:
            copy.wait_send()
        copies, own = coming[block]
        own.wait()
        for copy in copies:
            copy.wait()


def exchange_fit(main, side, materials):
    groups = lax.axis_size("energy")
    tiles = lax.axis_size("tile")
    tile_px = main.shape[-1]
    length = side.shape[-1]
    kinds = materials.shape[-1]
    rows = tile_px // groups
    blocks = tile_px // LANES
    vmem = pl.BlockSpec(memory_space=pltpu.VMEM)
    return pl.pallas_call(
        functools.partial(exchange_kernel, groups, tiles),
        out_shape=jax.ShapeDtypeStruct(main.shape, jnp.float32),
        in_specs=[pl.BlockSpec(memory_space=pltpu.SMEM), vmem, vmem],
        out_specs=vmem,
        scratch_shapes=[
            pltpu.SMEM((kinds * kinds,), jnp.float32),
            pltpu.VMEM((2, tile_px, length), jnp.float32),
            pltpu.VMEM((2, tile_px, length), jnp.float32),
            pltpu.VMEM((2, groups, rows, tile_px), jnp.float32),
            pltpu.VMEM((2, groups, rows, tile_px), jnp.float32),
            pltpu.SemaphoreType.DMA((2,)),
            pltpu.SemaphoreType.DMA((2, blocks, groups)),
            pltpu.SemaphoreType.DMA((2, blocks, groups)),
            pltpu.SemaphoreType.DMA((2, blocks)),
        ],
        compiler_params=pltpu.CompilerParams(
            collective_id=0, has_side_effects=True, vmem_limit_bytes=32 * 1024 * 1024
        ),
        name="exchange",
    )(materials.reshape(-1), main, side)


def body(object_tiles, probe_wave, measured, positions, materials):
    own_object = object_tiles[0, :, 0]
    tile_px = own_object.shape[-1]
    length = probe_wave.shape[-1]
    tile_count = lax.axis_size("tile")
    row_step = TILE_COLS % tile_count
    fold = row_step == 0
    right_strip = shifted(own_object[:, :, :length], "tile", -1)
    if fold:
        lower_strip = jnp.zeros((2, 8, LANES), jnp.float32)
    else:
        widened = jnp.concatenate([own_object[:, :length], right_strip[:, :length]], 2)
        lower_strip = shifted(widened, "tile", -row_step)
    shared = (own_object, probe_wave[0], measured[0, 0], positions[0], fold)
    (begun,) = patch_call(*shared)
    main, side, below = patch_call(*shared, margins=(right_strip, lower_strip, begun))
    if not fold:
        from_above = shifted(below, "tile", row_step)
        main = main.at[:, :length, :].add(from_above[:, :, :tile_px])
        side = side.at[:, :length, :].add(from_above[:, :, tile_px:])
    fitted = exchange_fit(main, side, materials)
    return fitted.reshape(1, 2, 1, tile_px, tile_px)


def solution(mesh):
    in_specs = (
        P("energy", None, "tile", None, None),
        P("energy", None, None, None),
        P("energy", "tile", None, None, None),
        P("tile", None, None),
        P(),
    )
    out_specs = P("energy", None, "tile", None, None)
    return jax.shard_map(body, mesh=mesh, in_specs=in_specs, out_specs=out_specs, check_vma=False)
```

```python
import functools
import math

import jax
import jax.numpy as jnp
import numpy as np
from jax import lax
from jax.experimental import pallas as pl
from jax.experimental.pallas import tpu as pltpu
from jax.sharding import PartitionSpec as P

TILE_COLS = 4
FIT_STEPS = 10
LANES = 128


amplitude_floor = 0.5


def shifted(value, axis, steps):
    count = lax.axis_size(axis)
    pairs = [(source, (source + steps) % count) for source in range(count)]
    return lax.ppermute(value, axis, pairs)


def fourier_parts(length):
    counter = np.arange(length, dtype=np.int64)
    angles = 2.0 * math.pi / length * (counter[:, None] * counter[None, :] % length)
    return jnp.asarray(
        np.stack([np.cos(angles), np.sin(angles)]).astype(np.float32).astype(jnp.bfloat16)
    )


def joined(top_left, top_right, bottom_left, bottom_right):
    return jnp.concatenate(
        [
            jnp.concatenate([top_left, top_right], 1),
            jnp.concatenate([bottom_left, bottom_right], 1),
        ],
        0,
    )


def transform(stacked, left_ref, right_ref):
    length = stacked.shape[0] // 2
    inner = jnp.dot(left_ref[...], stacked, preferred_element_type=jnp.float32)
    inner = inner.astype(jnp.bfloat16)
    beside = jnp.concatenate([inner[:length], inner[length:]], 1)
    outer = jnp.dot(beside, right_ref[...], preferred_element_type=jnp.float32) * (1.0 / length)
    return outer[:, :length], outer[:, length:]


def window(ref, part, row, block, shift, length):
    lane = lax.broadcasted_iota(jnp.int32, (length, LANES), 1)
    back = lax.rem(LANES - shift, LANES)
    tiles = [
        pltpu.roll(ref[part, block + at, pl.ds(row, length), :], back, 1)
        for at in range(length // LANES + 1)
    ]
    keep = lane < LANES - shift
    return jnp.concatenate(
        [jnp.where(keep, one, other) for one, other in zip(tiles[:-1], tiles[1:])], 1
    )


def add_window(ref, part, row, block, shift, term):
    length = term.shape[0]
    lane = lax.broadcasted_iota(jnp.int32, (length, LANES), 1)
    tiles = [pltpu.roll(term[:, at : at + LANES], shift, 1) for at in range(0, length, LANES)]
    keep = lane >= shift
    zero = jnp.zeros_like(tiles[0])
    for at, (one, other) in enumerate(zip(tiles + [zero], [zero] + tiles)):
        place = (part, block + at, pl.ds(row, length), slice(None))
        ref[place] = ref[place] + jnp.where(keep, one, other)


def patch_kernel(fold, inner, *refs):
    corners_ref, object_ref, measured_ref, probe_ref, fourier_ref = refs[:5]
    if inner:
        (gradient,) = refs[5:6]
        right_ref = lower_ref = None
        rest = refs[6:]
    else:
        right_ref, lower_ref, begun_ref, main_out, side_out, below_out = refs[5:11]
        gradient, *rest = refs[11:]
    field, tables, wave, change, terms, order, sems = rest
    tile_px = object_ref.shape[-1]
    length = probe_ref.shape[-1]
    count = measured_ref.shape[0]
    blocks = tile_px // LANES
    width = blocks + length // LANES
    top = pl.ds(0, tile_px)
    bottom = pl.ds(tile_px, length)
    moves = []
    for block in range(blocks if inner else width):
        ref, at = (object_ref, block) if block < blocks else (right_ref, block - blocks)
        columns = pl.ds(at * LANES, LANES)
        moves.append((ref.at[:, :, columns], field.at[:, block, top, :]))
        if fold and not inner and block < (tile_px - length) // LANES:
            continue
        if fold:
            source = ref.at[:, pl.ds(0, length), columns]
        elif not inner:
            source = lower_ref.at[:, :, pl.ds(block * LANES, LANES)]
        else:
            continue
        moves.append((source, field.at[:, block, bottom, :]))
    copies = [
        pltpu.make_async_copy(source, target, sems.at[number])
        for number, (source, target) in enumerate(moves)
    ]
    for copy in copies:
        copy.start()
    cosine = fourier_ref[0]
    sine = fourier_ref[1]
    tables[0] = joined(cosine, sine, -sine, cosine)
    tables[1] = joined(cosine, -sine, sine, cosine)
    if inner:
        gradient[...] = jnp.zeros_like(gradient)
    else:
        gradient[...] = begun_ref[...]
    terms[...] = jnp.zeros_like(terms)

    limit = tile_px - length

    def choose(number, found):
        order[found] = number
        within = corners_ref[number, 1] <= limit
        if not fold:
            within = jnp.logical_and(within, corners_ref[number, 0] <= limit)
        return found + jnp.where(within, int(inner), 1 - int(inner))

    total = lax.fori_loop(0, count, choose, 0)
    for copy in copies:
        copy.wait()

    def corner(turn):
        number = order[turn]
        row = corners_ref[number, 0]
        col = corners_ref[number, 1]
        block = col // LANES
        return number, row, block, col - block * LANES

    def gather(turn):
        _, row, block, shift = corner(turn)
        piece_real = window(field, 0, row, block, shift, length)
        piece_imag = window(field, 1, row, block, shift, length)
        probe_real = probe_ref[0]
        probe_imag = probe_ref[1]
        exit_real = probe_real * piece_real - probe_imag * piece_imag
        exit_imag = probe_real * piece_imag + probe_imag * piece_real
        wave[:length, :] = exit_real.astype(jnp.bfloat16)
        wave[length:, :] = exit_imag.astype(jnp.bfloat16)

    def scatter(turn):
        _, row, block, shift = corner(turn)
        add_window(gradient, 0, row, block, shift, terms[0])
        add_window(gradient, 1, row, block, shift, terms[1])

    def outward(turn):
        far_real, far_imag = transform(wave[...], tables.at[0], tables.at[1])
        square = far_real * far_real + far_imag * far_imag
        scale = lax.rsqrt(jnp.maximum(square, amplitude_floor * amplitude_floor))
        factor = measured_ref[order[turn]].astype(jnp.float32) * scale - 1.0
        return (factor * far_real).astype(jnp.bfloat16), (factor * far_imag).astype(jnp.bfloat16)

    def keep(parts):
        change[:length, :] = parts[0]
        change[length:, :] = parts[1]

    def homeward():
        back_real, back_imag = transform(change[...], tables.at[1], tables.at[0])
        probe_real = probe_ref[0]
        probe_imag = probe_ref[1]
        return (
            probe_real * back_real + probe_imag * back_imag,
            probe_real * back_imag - probe_imag * back_real,
        )

    def step(turn, carry):
        scatter(jnp.maximum(turn - 1, 0))
        parts = outward(turn + 1)
        back = homeward()
        keep(parts)
        gather(jnp.minimum(turn + 2, total - 1))
        terms[0] = back[0]
        terms[1] = back[1]
        return carry

    @pl.when(total > 0)
    def _():
        gather(0)
        keep(outward(0))
        gather(jnp.minimum(1, total - 1))
        lax.fori_loop(0, total - 1, step, 0)
        scatter(jnp.maximum(total - 2, 0))
        back = homeward()
        terms[0] = back[0]
        terms[1] = back[1]
        scatter(total - 1)

    if inner:
        return
    peak = jnp.max(probe_ref[0] * probe_ref[0] + probe_ref[1] * probe_ref[1])
    rows = 64

    def finish(wrapped, number, carry):
        place = (pl.ds(pl.multiple_of(number * rows, rows), rows), slice(None))
        beyond = pl.ds(pl.multiple_of(tile_px + number * rows, rows), rows)
        for part in range(2):
            for block in range(width):
                value = gradient[(part, block) + place]
                if wrapped:
                    value = value + gradient[part, block, beyond, :]
                share = value / peak
                if block < blocks:
                    columns = slice(block * LANES, (block + 1) * LANES)
                    main_out[part, place[0], columns] = field[(part, block) + place] + share
                else:
                    columns = slice((block - blocks) * LANES, (block - blocks + 1) * LANES)
                    side_out[part, place[0], columns] = share
        return carry

    lax.fori_loop(0, length // rows, functools.partial(finish, fold), 0)
    lax.fori_loop(length // rows, tile_px // rows, functools.partial(finish, False), 0)
    if fold:
        below_out[...] = jnp.zeros_like(below_out)
    else:
        for block in range(width):
            columns = slice(block * LANES, (block + 1) * LANES)
            below_out[:, :, columns] = gradient[:, block, tile_px:, :] / peak


def patch_call(own_object, probe, measured, corners, fold, margins=()):
    tile_px = own_object.shape[-1]
    length = probe.shape[-1]
    count = measured.shape[0]
    width = tile_px + length
    inner = not margins
    below = (2, 8, LANES) if fold else (2, length, width)
    vmem = pl.BlockSpec(memory_space=pltpu.VMEM)
    anywhere = pl.BlockSpec(memory_space=pl.ANY)
    sums = (2, width // LANES, width, LANES)
    if inner:
        shapes = [sums]
    else:
        shapes = [(2, tile_px, tile_px), (2, tile_px, length), below]
    scratch = [
        pltpu.VMEM(sums, jnp.float32),
        pltpu.VMEM((2, 2 * length, 2 * length), jnp.bfloat16),
        pltpu.VMEM((2 * length, length), jnp.bfloat16),
        pltpu.VMEM((2 * length, length), jnp.bfloat16),
        pltpu.VMEM((2, length, length), jnp.float32),
        pltpu.SMEM((count + 1,), jnp.int32),
        pltpu.SemaphoreType.DMA((2 * (width // LANES),)),
    ]
    if not inner:
        scratch = [pltpu.VMEM(sums, jnp.float32)] + scratch
    return pl.pallas_call(
        functools.partial(patch_kernel, fold, inner),
        out_shape=[jax.ShapeDtypeStruct(shape, jnp.float32) for shape in shapes],
        in_specs=[pl.BlockSpec(memory_space=pltpu.SMEM), anywhere, vmem, vmem, vmem]
        + ([] if inner else [anywhere, anywhere, vmem]),
        out_specs=[vmem] * len(shapes),
        scratch_shapes=scratch,
        compiler_params=pltpu.CompilerParams(vmem_limit_bytes=40 * 1024 * 1024),
        cost_estimate=pl.CostEstimate(
            flops=32 * count * length**3, bytes_accessed=16 * tile_px * tile_px, transcendentals=0
        ),
        name="patches_inner" if inner else "patches_outer",
    )(corners, own_object, measured, probe, fourier_parts(length), *margins)


def fit_scalars(materials_ref, energies, kinds):
    spectra = [
        [materials_ref[(part * energies + energy) * kinds + kind] for kind in range(kinds)]
        for part in range(2)
        for energy in range(energies)
    ]
    gram = [[None] * kinds for _ in range(kinds)]
    for one in range(kinds):
        for other in range(one, kinds):
            total = spectra[0][one] * spectra[0][other]
            for row in spectra[1:]:
                total = total + row[one] * row[other]
            gram[one][other] = total
            gram[other][one] = total
    trace = gram[0][0]
    for one in range(1, kinds):
        trace = trace + gram[one][one]
    return gram, trace


def fit_columns(materials_ref, step_ref, data, spectra, energies, kinds, rate, begin, wide):
    rows = data.shape[2]
    tall = 16 if rows % 16 == 0 else 8
    pairs = [(part, energy) for part in range(2) for energy in range(energies)]

    def chunk(number, carry):
        row = pl.multiple_of(number * tall, tall)
        place = (pl.ds(row, tall), pl.ds(begin, wide))
        target = [None] * kinds
        for part, energy in pairs:
            plane = data[(part, energy) + place]
            for kind in range(kinds):
                term = materials_ref[(part * energies + energy) * kinds + kind] * plane
                target[kind] = term if target[kind] is None else target[kind] + term
        target = [rate * value for value in target]
        current = [jnp.maximum(value, 0.0) for value in target]

        def descend(turn, current):
            following = []
            for one in range(kinds):
                total = target[one]
                for other in range(kinds):
                    total = total + step_ref[one * kinds + other] * current[other]
                following.append(jnp.maximum(total, 0.0))
            return following

        current = lax.fori_loop(1, FIT_STEPS, descend, current)
        for part, energy in pairs:
            total = None
            for kind in range(kinds):
                term = materials_ref[(part * energies + energy) * kinds + kind] * current[kind]
                total = term if total is None else total + term
            spectra[(part, energy) + place] = total
        return carry

    lax.fori_loop(0, rows // tall, chunk, 0)


def exchange_kernel(
    groups,
    tiles,
    materials_ref,
    main_ref,
    side_ref,
    out_ref,
    step_ref,
    margin,
    left,
    data,
    spectra,
    margin_sems,
    send_sems,
    recv_sems,
    own_sems,
):
    mesh_ids = pl.DeviceIdType.MESH
    me = lax.axis_index("energy")
    tile = lax.axis_index("tile")
    after = lax.rem(tile + 1, tiles)
    before = lax.rem(tile + tiles - 1, tiles)
    tile_px = main_ref.shape[-1]
    length = side_ref.shape[-1]
    rows = tile_px // groups
    kinds = materials_ref.shape[0] // (2 * groups)
    offsets = sorted(range(1, groups), key=lambda offset: abs(offset - groups // 2))
    peers = {offset: lax.rem(me + offset, groups) for offset in offsets}

    barrier = pltpu.get_barrier_semaphore()
    for neighbour in (after, before):
        pl.semaphore_signal(barrier, inc=1, device_id=(me, neighbour), device_id_type=mesh_ids)
    for offset in offsets:
        pl.semaphore_signal(
            barrier, inc=1, device_id=(peers[offset], tile), device_id_type=mesh_ids
        )

    pl.semaphore_wait(barrier, groups + 1)

    margin_copy = pltpu.make_async_remote_copy(
        src_ref=side_ref,
        dst_ref=margin,
        send_sem=margin_sems.at[0],
        recv_sem=margin_sems.at[1],
        device_id=(me, after),
        device_id_type=mesh_ids,
    )
    margin_copy.start()

    def rows_of(group):
        return pl.ds(pl.multiple_of(group * rows, rows), rows)

    def outward(block):
        columns = pl.ds(block * LANES, LANES)
        source = left if block * LANES < length else main_ref
        copies = [
            pltpu.make_async_remote_copy(
                src_ref=source.at[:, rows_of(peers[offset]), columns],
                dst_ref=data.at[:, me, :, columns],
                send_sem=send_sems.at[0, block, offset],
                recv_sem=recv_sems.at[0, block, offset],
                device_id=(peers[offset], tile),
                device_id_type=mesh_ids,
            )
            for offset in offsets
        ]
        own = pltpu.make_async_copy(
            source.at[:, rows_of(me), columns], data.at[:, me, :, columns], own_sems.at[0, block]
        )
        return copies, own

    def homeward(block):
        columns = pl.ds(block * LANES, LANES)
        copies = [
            pltpu.make_async_remote_copy(
                src_ref=spectra.at[:, peers[offset], :, columns],
                dst_ref=out_ref.at[:, rows_of(me), columns],
                send_sem=send_sems.at[1, block, offset],
                recv_sem=recv_sems.at[1, block, offset],
                device_id=(peers[offset], tile),
                device_id_type=mesh_ids,
            )
            for offset in offsets
        ]
        own = pltpu.make_async_copy(
            spectra.at[:, me, :, columns], out_ref.at[:, rows_of(me), columns], own_sems.at[1, block]
        )
        return copies, own

    def start(moves):
        for copy in moves[0]:
            copy.start()
        moves[1].start()

    blocks = tile_px // LANES
    early = [block for block in range(blocks) if block * LANES >= length]
    late = [block for block in range(blocks) if block * LANES < length]
    going = {}
    for block in early:
        going[block] = outward(block)
        start(going[block])

    gram, trace = fit_scalars(materials_ref, groups, kinds)
    rate = 1.0 / trace
    for one in range(kinds):
        for other in range(kinds):
            unit = 1.0 if one == other else 0.0
            step_ref[one * kinds + other] = unit - rate * gram[one][other]
    margin_copy.wait()
    for block in late:
        columns = slice(block * LANES, (block + 1) * LANES)
        left[:, :, columns] = main_ref[:, :, columns] + margin[:, :, columns]
    for block in late:
        going[block] = outward(block)
        start(going[block])
    coming = {}
    for block in early + late:
        copies, own = going[block]
        for copy in copies:
            copy.wait_recv()
        own.wait()
        fit_columns(
            materials_ref, step_ref, data, spectra, groups, kinds, rate, block * LANES, LANES
        )
        coming[block] = homeward(block)
        start(coming[block])
    for block in early + late:
        for copy in going[block][0]:
            copy.wait_send()
        copies, own = coming[block]
        own.wait()
        for copy in copies:
            copy.wait()


def exchange_fit(main, side, materials):
    groups = lax.axis_size("energy")
    tiles = lax.axis_size("tile")
    tile_px = main.shape[-1]
    length = side.shape[-1]
    kinds = materials.shape[-1]
    rows = tile_px // groups
    blocks = tile_px // LANES
    vmem = pl.BlockSpec(memory_space=pltpu.VMEM)
    return pl.pallas_call(
        functools.partial(exchange_kernel, groups, tiles),
        out_shape=jax.ShapeDtypeStruct(main.shape, jnp.float32),
        in_specs=[pl.BlockSpec(memory_space=pltpu.SMEM), vmem, vmem],
        out_specs=vmem,
        scratch_shapes=[
            pltpu.SMEM((kinds * kinds,), jnp.float32),
            pltpu.VMEM((2, tile_px, length), jnp.float32),
            pltpu.VMEM((2, tile_px, length), jnp.float32),
            pltpu.VMEM((2, groups, rows, tile_px), jnp.float32),
            pltpu.VMEM((2, groups, rows, tile_px), jnp.float32),
            pltpu.SemaphoreType.DMA((2,)),
            pltpu.SemaphoreType.DMA((2, blocks, groups)),
            pltpu.SemaphoreType.DMA((2, blocks, groups)),
            pltpu.SemaphoreType.DMA((2, blocks)),
        ],
        compiler_params=pltpu.CompilerParams(
            collective_id=0, has_side_effects=True, vmem_limit_bytes=32 * 1024 * 1024
        ),
        name="exchange",
    )(materials.reshape(-1), main, side)


def body(object_tiles, probe_wave, measured, positions, materials):
    own_object = object_tiles[0, :, 0]
    tile_px = own_object.shape[-1]
    length = probe_wave.shape[-1]
    tile_count = lax.axis_size("tile")
    row_step = TILE_COLS % tile_count
    fold = row_step == 0
    right_strip = shifted(own_object[:, :, :length], "tile", -1)
    if fold:
        lower_strip = jnp.zeros((2, 8, LANES), jnp.float32)
    else:
        widened = jnp.concatenate([own_object[:, :length], right_strip[:, :length]], 2)
        lower_strip = shifted(widened, "tile", -row_step)
    shared = (own_object, probe_wave[0], measured[0, 0], positions[0], fold)
    (begun,) = patch_call(*shared)
    main, side, below = patch_call(*shared, margins=(right_strip, lower_strip, begun))
    if not fold:
        from_above = shifted(below, "tile", row_step)
        main = main.at[:, :length, :].add(from_above[:, :, :tile_px])
        side = side.at[:, :length, :].add(from_above[:, :, tile_px:])
    fitted = exchange_fit(main, side, materials)
    return fitted.reshape(1, 2, 1, tile_px, tile_px)


def solution(mesh):
    in_specs = (
        P("energy", None, "tile", None, None),
        P("energy", None, None, None),
        P("energy", "tile", None, None, None),
        P("tile", None, None),
        P(),
    )
    out_specs = P("energy", None, "tile", None, None)
    return jax.shard_map(body, mesh=mesh, in_specs=in_specs, out_specs=out_specs, check_vma=False)
```
